256 devices in a mesh: gx: 64 (over z, x, core), gy: 4 (over y).
Axes of the slice: x: 4, y: 4, z: 8, core: 2. Of those that a mesh axis runs over, the one named last changes fastest.
Arguments:
- prior_warmth: float32 [16, 1024, 1024], P(None, 'gx', 'gy'), may hold values from -3 to 3
- prior_speed: float32 [16, 1024, 1024], P(None, 'gx', 'gy'), may hold values from -120 to 120
- energy_input: float32 [16, 1024, 1024], P(None, 'gx', 'gy'), may hold values from -120 to 120
Outputs:
- new_temperature: float32 [16, 1024, 1024], P(None, 'gx', 'gy')
- new_velocity: float32 [16, 1024, 1024], P(None, 'gx', 'gy')
The draws below stay inside these ranges and needn't reach their ends.
All inputs are finite; a program needn't handle non-finite values.
Results may differ from the reference program's by a relative error of at most 0.0003.
Values sent between devices are 32-bit elements; how exact they have to be, the bound alone decides.
No kernel may reach another device: no remote copies, remote signals or barrier semaphores. Data moves between devices by JAX's collectives and lax.ppermute only.
A program may use at most 64 MiB of HBM per device.

```python
import jax
import jax.numpy as jnp
from jax import lax

LAYER_COUNT = 16
WIDTH_COUNT = 1024
BREADTH_COUNT = 1024


def level_of(key, extent, split, least, top_value):
    def one(dim, blocks):
        steps = jax.random.uniform(jax.random.fold_in(jax.random.fold_in(key, 6), dim), (blocks,), jnp.float32, least / len(split), top_value / len(split))
        return jnp.repeat(jnp.exp(steps), extent[dim] // blocks).reshape((-1,) + (1,) * (len(extent) - dim - 1))

    level = one(*split[0])
    for cut in split[1:]:
        level = level * one(*cut)
    return level


def noise(stream_key, extent, scale, most, shards=(), held_as=jnp.bfloat16):
    array = scale * jax.random.normal(stream_key, extent, jnp.float32)
    if shards:
        array = array * level_of(stream_key, extent, shards, -0.22, 0.18)
    return jnp.clip(array, -most, most).astype(held_as)


def setup_inputs(seed: int = 0) -> dict:
    seeds = jax.random.split(jax.random.key(seed), 4)
    return {
        "prior_warmth": noise(seeds[0], (LAYER_COUNT, WIDTH_COUNT, BREADTH_COUNT), 1.0, 3.0, ((1, 64), (2, 4)), jnp.float32),
        "prior_speed": noise(seeds[1], (LAYER_COUNT, WIDTH_COUNT, BREADTH_COUNT), 20.0, 120.0, ((1, 64), (2, 4)), jnp.float32),
        "energy_input": noise(seeds[2], (LAYER_COUNT, WIDTH_COUNT, BREADTH_COUNT), 20.0, 120.0, ((1, 64), (2, 4)), jnp.float32),
    }


diffusivity_slope = 0.3
stickiness_slope = 0.8
lifting_push = 8.0
span_strength = 1500.0
cross_strength = 1500.0
depth_strength = 2.0


def thomas(below_band, centre_band, above_band, source):
    def forward(carried, row_values):
        ratio_old, partial_old = carried
        below_row, centre_row, above_row, source_row = row_values
        pivot_value = centre_row - below_row * ratio_old
        ratio_new = above_row / pivot_value
        partial_new = (source_row - below_row * partial_old) / pivot_value
        return (ratio_new, partial_new), (ratio_new, partial_new)

    start = (jnp.zeros_like(centre_band[0]), jnp.zeros_like(source[0]))
    _, (ratios, partials) = lax.scan(forward, start, (below_band, centre_band, above_band, source))

    def backward(following, row_values):
        ratio_row, partial_row = row_values
        answer = partial_row - ratio_row * following
        return answer, answer

    _, solved = lax.scan(backward, jnp.zeros_like(source[0]), (ratios, partials), reverse=True)
    return solved


def face_system(coefficient, line_axis, strength):
    length_along = coefficient.shape[line_axis]
    padded = jnp.pad(coefficient, [(1, 1) if position == line_axis else (0, 0) for position in range(coefficient.ndim)])
    face_values = strength * 0.5 * (lax.slice_in_dim(padded, 0, length_along + 1, axis=line_axis) + lax.slice_in_dim(padded, 1, length_along + 2, axis=line_axis))
    left_faces = lax.slice_in_dim(face_values, 0, length_along, axis=line_axis)
    right_faces = lax.slice_in_dim(face_values, 1, length_along + 1, axis=line_axis)
    return -left_faces, 1.0 + left_faces + right_faces, -right_faces


def line_solve(source, coefficient, line_axis, strength):
    below_band, centre_band, above_band = face_system(coefficient, line_axis, strength)
    moved_items = [jnp.moveaxis(member, line_axis, 0) for member in (below_band, centre_band, above_band, source)]
    line_shape = moved_items[0].shape
    flattened = [member.reshape(line_shape[0], -1) for member in moved_items]
    solved = thomas(flattened[0], flattened[1], flattened[2], flattened[3])
    return jnp.moveaxis(solved.reshape(line_shape), 0, line_axis)


def reference(prior_warmth, prior_speed, energy_input):
    heat_diffusivity = jnp.exp(diffusivity_slope * prior_warmth)
    stickiness_factor = jnp.exp(-stickiness_slope * prior_warmth)
    warmth_drive = prior_warmth + energy_input
    rising_drive = prior_speed + lifting_push * prior_warmth
    outputs = []
    for source, coefficient in ((warmth_drive, heat_diffusivity), (rising_drive, stickiness_factor)):
        first_pass = line_solve(source, coefficient, 1, span_strength)
        second_pass = line_solve(first_pass, coefficient, 2, cross_strength)
        outputs.append(line_solve(second_pass, coefficient, 0, depth_strength))
    return (outputs[0], outputs[1])
```

```python
import functools

import jax
import jax.numpy as jnp
from jax import lax
from jax.experimental import pallas as pl
from jax.experimental.pallas import tpu as pltpu
from jax.sharding import PartitionSpec as P

diffusivity_slope = 0.3
stickiness_slope = 0.8
lifting_push = 8.0
span_strength = 1500.0
cross_strength = 1500.0
depth_strength = 2.0

SLOPES = (diffusivity_slope, -stickiness_slope)
PAIRS = 2
LANES = 128
CHUNKS = 8
SENT = 8
SIDES = 2
CROSS_SENT = 7


def block_sweep(steps, coefficient_at, source_at, strength, opens, keep):
    half = 0.5 * strength
    q_first = q_now = coefficient_at(0)
    numerator = source_at(0)
    delta = 1.0 + opens * (half * q_first)
    weight = jnp.ones_like(q_now)
    first_part = jnp.zeros_like(q_now)
    first_reach = jnp.zeros_like(q_now)
    for step in range(steps):
        if step == steps - 1:
            inverse = 1.0 / delta
            partial = numerator * inverse
            reach = weight * inverse
            keep(step, inverse, partial, reach)
            first_part = first_part + weight * partial
            first_reach = first_reach + weight * reach
            return (first_part, partial, first_reach, reach, inverse, q_first, q_now)
        q_next = coefficient_at(step + 1)
        face = half * (q_now + q_next)
        inverse = 1.0 / (delta + face)
        ratio = face * inverse
        partial = numerator * inverse
        reach = weight * inverse
        keep(step, ratio, partial, reach)
        first_part = first_part + weight * partial
        first_reach = first_reach + weight * reach
        delta = 1.0 + delta * ratio
        weight = weight * ratio
        numerator = source_at(step + 1) + face * partial
        q_now = q_next


def block_return(steps, kept_at, flux_low, flux_high, give):
    answer = None
    for step in reversed(range(steps)):
        ratio, partial, reach = kept_at(step)
        fixed = partial + reach * flux_low
        answer = fixed - ratio * flux_high if answer is None else fixed + ratio * answer
        give(step, answer)


def interface_flux(values, strength, rows):
    first_part, last_part, first_reach, cross_reach, last_reach, q_first, q_last = values
    row = lax.broadcasted_iota(jnp.int32, first_part.shape, 0)

    def following(value):
        return jnp.where(row < rows - 1, pltpu.roll(value, rows - 1, 0), 0.0)

    face = 0.5 * strength * (q_last + following(q_first))
    scale = face / (1.0 + face * (last_reach + following(first_reach)))
    below = jnp.where(row > 0, scale * cross_reach, 0.0)
    above = scale * following(cross_reach)
    flux = scale * (last_part - following(first_part))
    step = 1
    while step < rows:
        below_low, above_low, flux_low = (pltpu.roll(v, step, 0) for v in (below, above, flux))
        below_high, above_high, flux_high = (
            pltpu.roll(v, rows - step, 0) for v in (below, above, flux)
        )
        inverse = 1.0 / (1.0 - below * above_low - above * below_high)
        flux = (flux + below * flux_low + above * flux_high) * inverse
        below = below * below_low * inverse
        above = above * above_high * inverse
        step *= 2
    return jnp.where(row > 0, pltpu.roll(flux, 1, 0), 0.0), flux


def wide(pieces):
    return jnp.concatenate(pieces, axis=1)


def span_forward(layers, rows, warm, speed, energy, send, ratios, partials, reaches):
    opens = (lax.axis_index("gx") == 0).astype(jnp.float32)

    def coefficient_at(i):
        warmth = warm[pl.ds(i, layers, stride=rows), :]
        return wide([jnp.exp(slope * warmth) for slope in SLOPES])

    def source_at(i):
        where = pl.ds(i, layers, stride=rows)
        warmth = warm[where, :]
        return wide([warmth + energy[where, :], speed[where, :] + lifting_push * warmth])

    def keep(i, ratio, partial, reach):
        where = slice(i * layers, (i + 1) * layers)
        ratios[where, :] = ratio
        partials[where, :] = partial
        reaches[where, :] = reach

    values = block_sweep(rows, coefficient_at, source_at, span_strength, opens, keep)
    for number, value in enumerate(values):
        for pair in range(PAIRS):
            send[pl.ds(pair * layers * SENT + number, layers, stride=SENT), :] = value[
                :, pair * LANES : (pair + 1) * LANES
            ]


def span_reduced(blocks, received, fluxes):
    values = [received[pl.ds(number, blocks, stride=SENT), :] for number in range(CROSS_SENT)]
    low, high = interface_flux(values, span_strength, blocks)
    fluxes[pl.ds(0, blocks, stride=SIDES), :] = low
    fluxes[pl.ds(1, blocks, stride=SIDES), :] = high


def span_back_cross_forward(
    layers, rows, breadth, warm, flux, ratios, partials, reaches,
    send, cross_ratios, cross_partials, cross_reaches, solved, turned, turned_warm,
):
    halves = breadth // LANES
    lines = layers * rows
    group = min(LANES, lines)
    groups = lines // group
    length = breadth // CHUNKS
    for h in range(halves):
        across = slice(h * LANES, (h + 1) * LANES)
        for g in range(groups):
            turned_warm[g * breadth + h * LANES : g * breadth + (h + 1) * LANES, :] = warm[
                g * group : (g + 1) * group, across
            ].T
    for h in range(halves):
        low, high = (
            wide([
                flux[pl.ds((h * PAIRS + pair) * layers * SIDES + side, layers, stride=SIDES), :]
                for pair in range(PAIRS)
            ])
            for side in range(SIDES)
        )

        def kept_at(i):
            where = slice((h * rows + i) * layers, (h * rows + i + 1) * layers)
            return ratios[where, :], partials[where, :], reaches[where, :]

        def give(i, answer):
            for pair in range(PAIRS):
                start = (h * PAIRS + pair) * lines + i
                solved[pl.ds(start, layers, stride=rows), :] = answer[
                    :, pair * LANES : (pair + 1) * LANES
                ]

        block_return(rows, kept_at, low, high, give)
        for pair in range(PAIRS):
            for g in range(groups):
                start = (h * PAIRS + pair) * lines + g * group
                target = (pair * groups + g) * breadth + h * LANES
                turned[target : target + LANES, :] = solved[start : start + group, :].T

    def chunk_row(ref, number, t):
        return ref[pl.ds(number * breadth + t, CHUNKS, stride=length), :]

    def coefficient_at(t):
        warmth = [chunk_row(turned_warm, g, t) for g in range(groups)]
        return wide([jnp.exp(slope * w) for slope in SLOPES for w in warmth])

    def source_at(t):
        return wide([chunk_row(turned, number, t) for number in range(PAIRS * groups)])

    def keep(t, ratio, partial, reach):
        where = slice(t * CHUNKS, (t + 1) * CHUNKS)
        cross_ratios[where, :] = ratio
        cross_partials[where, :] = partial
        cross_reaches[where, :] = reach

    leading = lax.broadcasted_iota(jnp.int32, (CHUNKS, PAIRS * lines), 0) == 0
    opens = jnp.where(leading, (lax.axis_index("gy") == 0).astype(jnp.float32), 0.0)
    values = block_sweep(length, coefficient_at, source_at, cross_strength, opens, keep)
    for number, value in enumerate(values):
        send[number * CHUNKS : (number + 1) * CHUNKS, :] = value


def cross_back_depth(
    layers, rows, breadth, parts, warm, received, ratios, partials, reaches,
    new_warmth, new_speed, fluxes, turned, solved, depth_ratios, depth_partials,
):
    halves = breadth // LANES
    lines = layers * rows
    group = min(LANES, lines)
    groups = lines // group
    length = breadth // CHUNKS
    own = lax.axis_index("gy")
    for pair in range(PAIRS):
        span = slice(pair * lines, (pair + 1) * lines)
        values = []
        for number in range(CROSS_SENT):
            starts = [(d * CROSS_SENT + number) * CHUNKS for d in range(parts)]
            pieces = [received[start : start + CHUNKS, span] for start in starts]
            values.append(jnp.concatenate(pieces, axis=0))
        low, high = interface_flux(values, cross_strength, parts * CHUNKS)
        fluxes[0 : parts * CHUNKS, span] = low
        fluxes[parts * CHUNKS :, span] = high
    low = fluxes[pl.ds(pl.multiple_of(own * CHUNKS, CHUNKS), CHUNKS), :]
    high = fluxes[pl.ds(pl.multiple_of((parts + own) * CHUNKS, CHUNKS), CHUNKS), :]

    def kept_at(t):
        where = slice(t * CHUNKS, (t + 1) * CHUNKS)
        return ratios[where, :], partials[where, :], reaches[where, :]

    def give(t, answer):
        for number in range(PAIRS * groups):
            turned[pl.ds(number * breadth + t, CHUNKS, stride=length), :] = answer[
                :, number * group : (number + 1) * group
            ]

    block_return(length, kept_at, low, high, give)
    for number in range(PAIRS * groups):
        for h in range(halves):
            start = number * breadth + h * LANES
            solved[number * group : (number + 1) * group, h * LANES : (h + 1) * LANES] = turned[
                start : start + LANES, :
            ].T
    for pair, out in enumerate((new_warmth, new_speed)):
        half = 0.5 * depth_strength

        def coefficient_at(z):
            return jnp.exp(SLOPES[pair] * warm[z * rows : (z + 1) * rows, :])

        def source_at(z):
            return solved[pair * lines + z * rows : pair * lines + (z + 1) * rows, :]

        q_now = coefficient_at(0)
        numerator = source_at(0)
        delta = 1.0 + half * q_now
        for z in range(layers - 1):
            where = slice(z * rows, (z + 1) * rows)
            q_next = coefficient_at(z + 1)
            face = half * (q_now + q_next)
            inverse = 1.0 / (delta + face)
            ratio = face * inverse
            partial = numerator * inverse
            depth_ratios[where, :] = ratio
            depth_partials[where, :] = partial
            delta = 1.0 + delta * ratio
            numerator = source_at(z + 1) + face * partial
            q_now = q_next
        answer = numerator / (delta + half * q_now)
        out[(layers - 1) * rows : layers * rows, :] = answer
        for z in reversed(range(layers - 1)):
            where = slice(z * rows, (z + 1) * rows)
            answer = depth_partials[where, :] + depth_ratios[where, :] * answer
            out[where, :] = answer


def shaped(*shape):
    return jax.ShapeDtypeStruct(shape, jnp.float32)


def held(*shape):
    return pltpu.VMEM(shape, jnp.float32)


INTERPRET = False


def body(prior_warmth, prior_speed, energy_input):
    layers, rows, breadth = prior_warmth.shape
    lines = layers * rows
    halves = breadth // LANES
    group = min(LANES, lines)
    blocks = lax.axis_size("gx")
    parts = lax.axis_size("gy")
    warm, speed, energy = (v.reshape(lines, breadth) for v in (prior_warmth, prior_speed, energy_input))
    kept = shaped(halves * lines, PAIRS * LANES)
    column_spec = pl.BlockSpec((lines, LANES), lambda h: (0, h))
    kept_spec = pl.BlockSpec((lines, PAIRS * LANES), lambda h: (h, 0))
    send_rows = PAIRS * layers * SENT
    send, ratios, partials, reaches = pl.pallas_call(
        functools.partial(span_forward, layers, rows),
        grid=(halves,),
        in_specs=[column_spec] * 3,
        out_specs=(pl.BlockSpec((send_rows, LANES), lambda h: (h, 0)), kept_spec, kept_spec, kept_spec),
        out_shape=(shaped(blocks * SENT, LANES), kept, kept, kept),
        name="span_forward",
        interpret=INTERPRET,
    )(warm, speed, energy)
    received = lax.all_to_all(
        send.reshape(blocks, SENT, LANES), "gx", split_axis=0, concat_axis=0, tiled=True
    )
    flux = pl.pallas_call(
        functools.partial(span_reduced, blocks),
        out_shape=shaped(blocks * SIDES, LANES),
        name="span_reduced",
        interpret=INTERPRET,
    )(received.reshape(blocks * SENT, LANES))
    flux = lax.all_to_all(
        flux.reshape(blocks, SIDES, LANES), "gx", split_axis=0, concat_axis=0, tiled=True
    ).reshape(blocks * SIDES, LANES)
    kept = shaped(breadth, PAIRS * lines)
    send, cross_ratios, cross_partials, cross_reaches = pl.pallas_call(
        functools.partial(span_back_cross_forward, layers, rows, breadth),
        out_shape=(shaped(CROSS_SENT * CHUNKS, PAIRS * lines), kept, kept, kept),
        scratch_shapes=[
            held(halves * PAIRS * lines, LANES),
            held(PAIRS * lines // group * breadth, group),
            held(lines // group * breadth, group),
        ],
        name="span_back_cross_forward",
        interpret=INTERPRET,
    )(warm, flux, ratios, partials, reaches)
    spread = jnp.broadcast_to(send[None], (parts,) + send.shape)
    gathered = lax.all_to_all(spread, "gy", split_axis=0, concat_axis=0, tiled=True)
    out = shaped(lines, breadth)
    finished = pl.pallas_call(
        functools.partial(cross_back_depth, layers, rows, breadth, parts),
        out_shape=(out, out),
        scratch_shapes=[
            held(2 * parts * CHUNKS, PAIRS * lines),
            held(PAIRS * lines // group * breadth, group),
            held(PAIRS * lines, breadth),
            held(lines, breadth),
            held(lines, breadth),
        ],
        name="cross_back_depth",
        interpret=INTERPRET,
    )(
        warm, gathered.reshape(parts * CROSS_SENT * CHUNKS, PAIRS * lines),
        cross_ratios, cross_partials, cross_reaches,
    )
    return tuple(v.reshape(layers, rows, breadth) for v in finished)


def solution(mesh):
    in_specs = (P(None, "gx", "gy"), P(None, "gx", "gy"), P(None, "gx", "gy"))
    out_specs = (P(None, "gx", "gy"), P(None, "gx", "gy"))
    return jax.shard_map(body, mesh=mesh, in_specs=in_specs, out_specs=out_specs, check_vma=False)
```

```python
import functools

import jax
import jax.numpy as jnp
from jax import lax
from jax.experimental import pallas as pl
from jax.experimental.pallas import tpu as pltpu
from jax.sharding import PartitionSpec as P

diffusivity_slope = 0.3
stickiness_slope = 0.8
lifting_push = 8.0
span_strength = 1500.0
cross_strength = 1500.0
depth_strength = 2.0

SLOPES = (diffusivity_slope, -stickiness_slope)
PAIRS = 2
LANES = 128
CHUNKS = 8
SENT = 8
SIDES = 2
CROSS_SENT = 7


def block_sweep(steps, coefficient_at, source_at, strength, opens, keep):
    half = 0.5 * strength
    q_first = q_now = coefficient_at(0)
    numerator = source_at(0)
    delta = 1.0 + opens * (half * q_first)
    weight = jnp.ones_like(q_now)
    first_part = jnp.zeros_like(q_now)
    first_reach = jnp.zeros_like(q_now)
    for step in range(steps):
        if step == steps - 1:
            inverse = 1.0 / delta
            partial = numerator * inverse
            reach = weight * inverse
            keep(step, inverse, partial, reach)
            first_part = first_part + weight * partial
            first_reach = first_reach + weight * reach
            return (first_part, partial, first_reach, reach, inverse, q_first, q_now)
        q_next = coefficient_at(step + 1)
        face = half * (q_now + q_next)
        inverse = 1.0 / (delta + face)
        ratio = face * inverse
        partial = numerator * inverse
        reach = weight * inverse
        keep(step, ratio, partial, reach)
        first_part = first_part + weight * partial
        first_reach = first_reach + weight * reach
        delta = 1.0 + delta * ratio
        weight = weight * ratio
        numerator = source_at(step + 1) + face * partial
        q_now = q_next


def block_return(steps, kept_at, flux_low, flux_high, give):
    answer = None
    for step in reversed(range(steps)):
        ratio, partial, reach = kept_at(step)
        fixed = partial + reach * flux_low
        answer = fixed - ratio * flux_high if answer is None else fixed + ratio * answer
        give(step, answer)


def interface_flux(values, strength, rows):
    first_part, last_part, first_reach, cross_reach, last_reach, q_first, q_last = values
    row = lax.broadcasted_iota(jnp.int32, first_part.shape, 0)

    def following(value):
        return jnp.where(row < rows - 1, pltpu.roll(value, rows - 1, 0), 0.0)

    face = 0.5 * strength * (q_last + following(q_first))
    scale = face / (1.0 + face * (last_reach + following(first_reach)))
    below = jnp.where(row > 0, scale * cross_reach, 0.0)
    above = scale * following(cross_reach)
    flux = scale * (last_part - following(first_part))
    step = 1
    while step < rows:
        below_low, above_low, flux_low = (pltpu.roll(v, step, 0) for v in (below, above, flux))
        below_high, above_high, flux_high = (
            pltpu.roll(v, rows - step, 0) for v in (below, above, flux)
        )
        inverse = 1.0 / (1.0 - below * above_low - above * below_high)
        flux = (flux + below * flux_low + above * flux_high) * inverse
        below = below * below_low * inverse
        above = above * above_high * inverse
        step *= 2
    return jnp.where(row > 0, pltpu.roll(flux, 1, 0), 0.0), flux


def merge_chunks(values, strength, rows):
    first_part, last_part, first_reach, cross_reach, last_reach, q_first, q_last = values
    row = lax.broadcasted_iota(jnp.int32, first_part.shape, 0)

    def following(value):
        return pltpu.roll(value, rows - 1, 0)

    def preceding(value):
        return pltpu.roll(value, 1, 0)

    face = 0.5 * strength * (q_last + following(q_first))
    scale = face / (1.0 + face * (last_reach + following(first_reach)))
    scale = jnp.where(row < rows - 1, scale, 0.0)
    below = scale * cross_reach
    above = scale * following(cross_reach)
    fixed = scale * (last_part - following(first_part))
    by_low = jnp.where(row == 0, below, 0.0)
    by_high = jnp.where(row == rows - 2, above, 0.0)
    below = jnp.where(row > 0, below, 0.0)
    above = jnp.where(row < rows - 2, above, 0.0)
    step = 1
    while step < rows:
        lows = [pltpu.roll(v, step, 0) for v in (below, above, fixed, by_low, by_high)]
        highs = [pltpu.roll(v, rows - step, 0) for v in (below, above, fixed, by_low, by_high)]
        inverse = 1.0 / (1.0 - below * lows[1] - above * highs[0])
        fixed, by_low, by_high = (
            (now + below * low + above * high) * inverse
            for now, low, high in zip((fixed, by_low, by_high), lows[2:], highs[2:])
        )
        below = below * lows[0] * inverse
        above = above * highs[1] * inverse
        step *= 2
    by_high = jnp.where(row < rows - 1, by_high, 1.0)
    merged = (
        (first_part - cross_reach * fixed, 0),
        (last_part + cross_reach * preceding(fixed), rows - 1),
        (first_reach - cross_reach * by_low, 0),
        (cross_reach * preceding(by_low), rows - 1),
        (last_reach - cross_reach * preceding(by_high), rows - 1),
        (q_first, 0),
        (q_last, rows - 1),
    )
    return (fixed, by_low, by_high), [value[at : at + 1, :] for value, at in merged]


def own_flux(parts_values, strength, own):
    half = 0.5 * strength
    ratios, fluxes = [], []
    for j, (_, last_part, _, cross_reach, last_reach, _, q_last) in enumerate(parts_values):
        if j + 1 < len(parts_values):
            first_part, _, first_reach, next_cross, _, q_first, _ = parts_values[j + 1]
            face = half * (q_last + q_first)
            centre = 1.0 + face * (last_reach + first_reach)
            right = face * (last_part - first_part)
            above = face * next_cross
        else:
            face = half * q_last
            centre = 1.0 + face * last_reach
            right = face * last_part
            above = None
        if j:
            below = face * cross_reach
            centre = centre - below * ratios[-1]
            right = right + below * fluxes[-1]
        inverse = 1.0 / centre
        fluxes.append(right * inverse)
        ratios.append(None if above is None else above * inverse)
    high = flux = fluxes[-1]
    low = jnp.zeros_like(flux)
    for j in reversed(range(len(fluxes) - 1)):
        flux = fluxes[j] + ratios[j] * flux
        low = jnp.where(own == j + 1, flux, low)
        high = jnp.where(own == j, flux, high)
    return low, high


def wide(pieces):
    return jnp.concatenate(pieces, axis=1)


def span_forward(layers, rows, warm, speed, energy, send, ratios, partials, reaches):
    opens = (lax.axis_index("gx") == 0).astype(jnp.float32)

    def coefficient_at(i):
        warmth = warm[pl.ds(i, layers, stride=rows), :]
        return wide([jnp.exp(slope * warmth) for slope in SLOPES])

    def source_at(i):
        where = pl.ds(i, layers, stride=rows)
        warmth = warm[where, :]
        return wide([warmth + energy[where, :], speed[where, :] + lifting_push * warmth])

    def keep(i, ratio, partial, reach):
        where = slice(i * layers, (i + 1) * layers)
        ratios[where, :] = ratio
        partials[where, :] = partial
        reaches[where, :] = reach

    values = block_sweep(rows, coefficient_at, source_at, span_strength, opens, keep)
    for number, value in enumerate(values):
        for pair in range(PAIRS):
            send[pl.ds(pair * layers * SENT + number, layers, stride=SENT), :] = value[
                :, pair * LANES : (pair + 1) * LANES
            ]


def span_reduced(blocks, received, fluxes):
    values = [received[pl.ds(number, blocks, stride=SENT), :] for number in range(CROSS_SENT)]
    low, high = interface_flux(values, span_strength, blocks)
    fluxes[pl.ds(0, blocks, stride=SIDES), :] = low
    fluxes[pl.ds(1, blocks, stride=SIDES), :] = high


def span_back_cross_forward(
    layers, rows, breadth, warm, flux, ratios, partials, reaches,
    send, chunk_fluxes, cross_ratios, cross_partials, cross_reaches, solved, turned, turned_warm,
):
    halves = breadth // LANES
    lines = layers * rows
    group = min(LANES, lines)
    groups = lines // group
    length = breadth // CHUNKS
    for h in range(halves):
        across = slice(h * LANES, (h + 1) * LANES)
        for g in range(groups):
            turned_warm[g * breadth + h * LANES : g * breadth + (h + 1) * LANES, :] = warm[
                g * group : (g + 1) * group, across
            ].T
    for h in range(halves):
        low, high = (
            wide([
                flux[pl.ds((h * PAIRS + pair) * layers * SIDES + side, layers, stride=SIDES), :]
                for pair in range(PAIRS)
            ])
            for side in range(SIDES)
        )

        def kept_at(i):
            where = slice((h * rows + i) * layers, (h * rows + i + 1) * layers)
            return ratios[where, :], partials[where, :], reaches[where, :]

        def give(i, answer):
            for pair in range(PAIRS):
                start = (h * PAIRS + pair) * lines + i
                solved[pl.ds(start, layers, stride=rows), :] = answer[
                    :, pair * LANES : (pair + 1) * LANES
                ]

        block_return(rows, kept_at, low, high, give)
        for pair in range(PAIRS):
            for g in range(groups):
                start = (h * PAIRS + pair) * lines + g * group
                target = (pair * groups + g) * breadth + h * LANES
                turned[target : target + LANES, :] = solved[start : start + group, :].T

    def chunk_row(ref, number, t):
        return ref[pl.ds(number * breadth + t, CHUNKS, stride=length), :]

    def coefficient_at(t):
        warmth = [chunk_row(turned_warm, g, t) for g in range(groups)]
        return wide([jnp.exp(slope * w) for slope in SLOPES for w in warmth])

    def source_at(t):
        return wide([chunk_row(turned, number, t) for number in range(PAIRS * groups)])

    def keep(t, ratio, partial, reach):
        where = slice(t * CHUNKS, (t + 1) * CHUNKS)
        cross_ratios[where, :] = ratio
        cross_partials[where, :] = partial
        cross_reaches[where, :] = reach

    leading = lax.broadcasted_iota(jnp.int32, (CHUNKS, PAIRS * lines), 0) == 0
    opens = jnp.where(leading, (lax.axis_index("gy") == 0).astype(jnp.float32), 0.0)
    values = block_sweep(length, coefficient_at, source_at, cross_strength, opens, keep)
    linear, merged = merge_chunks(values, cross_strength, CHUNKS)
    for number, value in enumerate(linear):
        chunk_fluxes[number * CHUNKS : (number + 1) * CHUNKS, :] = value
    for number, value in enumerate(merged + merged[-1:]):
        send[number : number + 1, :] = value


def cross_back_depth(
    layers, rows, breadth, parts, warm, *refs
):
    received, refs = refs[:parts], refs[parts:]
    chunk_fluxes, ratios, partials, reaches, new_warmth, new_speed = refs[:6]
    ordered, turned, solved, depth_ratios, depth_partials = refs[6:]
    halves = breadth // LANES
    lines = layers * rows
    group = min(LANES, lines)
    groups = lines // group
    length = breadth // CHUNKS
    own = lax.axis_index("gy")
    for steps in range(parts):
        slot = lax.rem(own + parts - steps, parts)
        ordered[pl.ds(pl.multiple_of(slot * SENT, SENT), SENT), :] = received[steps][...]
    parts_values = [
        [ordered[d * SENT + number : d * SENT + number + 1, :] for number in range(CROSS_SENT)]
        for d in range(parts)
    ]
    end_low, end_high = own_flux(parts_values, cross_strength, own)
    fixed, by_low, by_high = (
        chunk_fluxes[number * CHUNKS : (number + 1) * CHUNKS, :] for number in range(3)
    )
    high = fixed + by_low * end_low + by_high * end_high
    row = lax.broadcasted_iota(jnp.int32, high.shape, 0)
    low = jnp.where(row > 0, pltpu.roll(high, 1, 0), end_low)

    def kept_at(t):
        where = slice(t * CHUNKS, (t + 1) * CHUNKS)
        return ratios[where, :], partials[where, :], reaches[where, :]

    def give(t, answer):
        for number in range(PAIRS * groups):
            turned[pl.ds(number * breadth + t, CHUNKS, stride=length), :] = answer[
                :, number * group : (number + 1) * group
            ]

    block_return(length, kept_at, low, high, give)
    for number in range(PAIRS * groups):
        for h in range(halves):
            start = number * breadth + h * LANES
            solved[number * group : (number + 1) * group, h * LANES : (h + 1) * LANES] = turned[
                start : start + LANES, :
            ].T
    for pair, out in enumerate((new_warmth, new_speed)):
        half = 0.5 * depth_strength

        def coefficient_at(z):
            return jnp.exp(SLOPES[pair] * warm[z * rows : (z + 1) * rows, :])

        def source_at(z):
            return solved[pair * lines + z * rows : pair * lines + (z + 1) * rows, :]

        q_now = coefficient_at(0)
        numerator = source_at(0)
        delta = 1.0 + half * q_now
        for z in range(layers - 1):
            where = slice(z * rows, (z + 1) * rows)
            q_next = coefficient_at(z + 1)
            face = half * (q_now + q_next)
            inverse = 1.0 / (delta + face)
            ratio = face * inverse
            partial = numerator * inverse
            depth_ratios[where, :] = ratio
            depth_partials[where, :] = partial
            delta = 1.0 + delta * ratio
            numerator = source_at(z + 1) + face * partial
            q_now = q_next
        answer = numerator / (delta + half * q_now)
        out[(layers - 1) * rows : layers * rows, :] = answer
        for z in reversed(range(layers - 1)):
            where = slice(z * rows, (z + 1) * rows)
            answer = depth_partials[where, :] + depth_ratios[where, :] * answer
            out[where, :] = answer


def shaped(*shape):
    return jax.ShapeDtypeStruct(shape, jnp.float32)


def held(*shape):
    return pltpu.VMEM(shape, jnp.float32)


INTERPRET = False


def body(prior_warmth, prior_speed, energy_input):
    layers, rows, breadth = prior_warmth.shape
    lines = layers * rows
    halves = breadth // LANES
    group = min(LANES, lines)
    blocks = lax.axis_size("gx")
    parts = lax.axis_size("gy")
    warm, speed, energy = (v.reshape(lines, breadth) for v in (prior_warmth, prior_speed, energy_input))
    kept = shaped(halves * lines, PAIRS * LANES)
    column_spec = pl.BlockSpec((lines, LANES), lambda h: (0, h))
    kept_spec = pl.BlockSpec((lines, PAIRS * LANES), lambda h: (h, 0))
    send_rows = PAIRS * layers * SENT
    send, ratios, partials, reaches = pl.pallas_call(
        functools.partial(span_forward, layers, rows),
        grid=(halves,),
        in_specs=[column_spec] * 3,
        out_specs=(pl.BlockSpec((send_rows, LANES), lambda h: (h, 0)), kept_spec, kept_spec, kept_spec),
        out_shape=(shaped(blocks * SENT, LANES), kept, kept, kept),
        name="span_forward",
        interpret=INTERPRET,
    )(warm, speed, energy)
    received = lax.all_to_all(
        send.reshape(blocks, SENT, LANES), "gx", split_axis=0, concat_axis=0, tiled=True
    )
    flux = pl.pallas_call(
        functools.partial(span_reduced, blocks),
        out_shape=shaped(blocks * SIDES, LANES),
        name="span_reduced",
        interpret=INTERPRET,
    )(received.reshape(blocks * SENT, LANES))
    flux = lax.all_to_all(
        flux.reshape(blocks, SIDES, LANES), "gx", split_axis=0, concat_axis=0, tiled=True
    ).reshape(blocks * SIDES, LANES)
    kept = shaped(breadth, PAIRS * lines)
    send, chunk_fluxes, *cross_kept = pl.pallas_call(
        functools.partial(span_back_cross_forward, layers, rows, breadth),
        out_shape=(
            shaped(SENT, PAIRS * lines), shaped(3 * CHUNKS, PAIRS * lines), kept, kept, kept,
        ),
        scratch_shapes=[
            held(halves * PAIRS * lines, LANES),
            held(PAIRS * lines // group * breadth, group),
            held(lines // group * breadth, group),
        ],
        name="span_back_cross_forward",
        interpret=INTERPRET,
    )(warm, flux, ratios, partials, reaches)
    received = [send] + [
        lax.ppermute(send, "gy", [(i, (i + steps) % parts) for i in range(parts)])
        for steps in range(1, parts)
    ]
    out = shaped(lines, breadth)
    finished = pl.pallas_call(
        functools.partial(cross_back_depth, layers, rows, breadth, parts),
        out_shape=(out, out),
        scratch_shapes=[
            held(parts * SENT, PAIRS * lines),
            held(PAIRS * lines // group * breadth, group),
            held(PAIRS * lines, breadth),
            held(lines, breadth),
            held(lines, breadth),
        ],
        name="cross_back_depth",
        interpret=INTERPRET,
    )(warm, *received, chunk_fluxes, *cross_kept)
    return tuple(v.reshape(layers, rows, breadth) for v in finished)


def solution(mesh):
    in_specs = (P(None, "gx", "gy"), P(None, "gx", "gy"), P(None, "gx", "gy"))
    out_specs = (P(None, "gx", "gy"), P(None, "gx", "gy"))
    return jax.shard_map(body, mesh=mesh, in_specs=in_specs, out_specs=out_specs, check_vma=False)
```

```python
import functools

import jax
import jax.numpy as jnp
from jax import lax
from jax.experimental import pallas as pl
from jax.experimental.pallas import tpu as pltpu
from jax.sharding import PartitionSpec as P

diffusivity_slope = 0.3
stickiness_slope = 0.8
lifting_push = 8.0
span_strength = 1500.0
cross_strength = 1500.0
depth_strength = 2.0

SLOPES = (diffusivity_slope, -stickiness_slope)
PAIRS = 2
LANES = 128
CHUNKS = 8
SENT = 8
SIDES = 2
ROOM = 24 * 2**20
CROSS_SENT = 7


def block_sweep(steps, coefficient_at, source_at, strength, opens, keep):
    half = 0.5 * strength
    q_first = q_now = coefficient_at(0)
    numerator = source_at(0)
    delta = 1.0 + opens * (half * q_first)
    weight = jnp.ones_like(q_now)
    first_part = jnp.zeros_like(q_now)
    first_reach = jnp.zeros_like(q_now)
    for step in range(steps):
        if step == steps - 1:
            inverse = 1.0 / delta
            partial = numerator * inverse
            reach = weight * inverse
            keep(step, inverse, partial, reach)
            first_part = first_part + weight * partial
            first_reach = first_reach + weight * reach
            return (first_part, partial, first_reach, reach, inverse, q_first, q_now)
        q_next = coefficient_at(step + 1)
        face = half * (q_now + q_next)
        inverse = 1.0 / (delta + face)
        ratio = face * inverse
        partial = numerator * inverse
        reach = weight * inverse
        keep(step, ratio, partial, reach)
        first_part = first_part + weight * partial
        first_reach = first_reach + weight * reach
        delta = 1.0 + delta * ratio
        weight = weight * ratio
        numerator = source_at(step + 1) + face * partial
        q_now = q_next


def block_return(steps, kept_at, flux_low, flux_high, give):
    answer = None
    for step in reversed(range(steps)):
        ratio, partial, reach = kept_at(step)
        fixed = partial + reach * flux_low
        answer = fixed - ratio * flux_high if answer is None else fixed + ratio * answer
        give(step, answer)


def interface_flux(values, strength, rows):
    first_part, last_part, first_reach, cross_reach, last_reach, q_first, q_last = values
    row = lax.broadcasted_iota(jnp.int32, first_part.shape, 0)

    def following(value):
        return jnp.where(row < rows - 1, pltpu.roll(value, rows - 1, 0), 0.0)

    face = 0.5 * strength * (q_last + following(q_first))
    scale = face / (1.0 + face * (last_reach + following(first_reach)))
    below = jnp.where(row > 0, scale * cross_reach, 0.0)
    above = scale * following(cross_reach)
    flux = scale * (last_part - following(first_part))
    step = 1
    while step < rows:
        below_low, above_low, flux_low = (pltpu.roll(v, step, 0) for v in (below, above, flux))
        below_high, above_high, flux_high = (
            pltpu.roll(v, rows - step, 0) for v in (below, above, flux)
        )
        inverse = 1.0 / (1.0 - below * above_low - above * below_high)
        flux = (flux + below * flux_low + above * flux_high) * inverse
        below = below * below_low * inverse
        above = above * above_high * inverse
        step *= 2
    return jnp.where(row > 0, pltpu.roll(flux, 1, 0), 0.0), flux


def merge_chunks(values, strength, rows):
    first_part, last_part, first_reach, cross_reach, last_reach, q_first, q_last = values
    row = lax.broadcasted_iota(jnp.int32, first_part.shape, 0)

    def following(value):
        return pltpu.roll(value, rows - 1, 0)

    def preceding(value):
        return pltpu.roll(value, 1, 0)

    face = 0.5 * strength * (q_last + following(q_first))
    scale = face / (1.0 + face * (last_reach + following(first_reach)))
    scale = jnp.where(row < rows - 1, scale, 0.0)
    below = scale * cross_reach
    above = scale * following(cross_reach)
    fixed = scale * (last_part - following(first_part))
    by_low = jnp.where(row == 0, below, 0.0)
    by_high = jnp.where(row == rows - 2, above, 0.0)
    below = jnp.where(row > 0, below, 0.0)
    above = jnp.where(row < rows - 2, above, 0.0)
    step = 1
    while step < rows:
        lows = [pltpu.roll(v, step, 0) for v in (below, above, fixed, by_low, by_high)]
        highs = [pltpu.roll(v, rows - step, 0) for v in (below, above, fixed, by_low, by_high)]
        inverse = 1.0 / (1.0 - below * lows[1] - above * highs[0])
        fixed, by_low, by_high = (
            (now + below * low + above * high) * inverse
            for now, low, high in zip((fixed, by_low, by_high), lows[2:], highs[2:])
        )
        below = below * lows[0] * inverse
        above = above * highs[1] * inverse
        step *= 2
    by_high = jnp.where(row < rows - 1, by_high, 1.0)
    merged = (
        (first_part - cross_reach * fixed, 0),
        (last_part + cross_reach * preceding(fixed), rows - 1),
        (first_reach - cross_reach * by_low, 0),
        (cross_reach * preceding(by_low), rows - 1),
        (last_reach - cross_reach * preceding(by_high), rows - 1),
        (q_first, 0),
        (q_last, rows - 1),
    )
    return (fixed, by_low, by_high), [value[at : at + 1, :] for value, at in merged]


def own_flux(parts_values, strength, own):
    half = 0.5 * strength
    ratios, fluxes = [], []
    for j, (_, last_part, _, cross_reach, last_reach, _, q_last) in enumerate(parts_values):
        if j + 1 < len(parts_values):
            first_part, _, first_reach, next_cross, _, q_first, _ = parts_values[j + 1]
            face = half * (q_last + q_first)
            centre = 1.0 + face * (last_reach + first_reach)
            right = face * (last_part - first_part)
            above = face * next_cross
        else:
            face = half * q_last
            centre = 1.0 + face * last_reach
            right = face * last_part
            above = None
        if j:
            below = face * cross_reach
            centre = centre - below * ratios[-1]
            right = right + below * fluxes[-1]
        inverse = 1.0 / centre
        fluxes.append(right * inverse)
        ratios.append(None if above is None else above * inverse)
    high = flux = fluxes[-1]
    low = jnp.zeros_like(flux)
    for j in reversed(range(len(fluxes) - 1)):
        flux = fluxes[j] + ratios[j] * flux
        low = jnp.where(own == j + 1, flux, low)
        high = jnp.where(own == j, flux, high)
    return low, high


def wide(pieces):
    return jnp.concatenate(pieces, axis=1)


def span_forward(layers, rows, warm, speed, energy, send, ratios, partials, reaches):
    opens = (lax.axis_index("gx") == 0).astype(jnp.float32)

    def coefficient_at(i):
        warmth = warm[pl.ds(i, layers, stride=rows), :]
        return wide([jnp.exp(slope * warmth) for slope in SLOPES])

    def source_at(i):
        where = pl.ds(i, layers, stride=rows)
        warmth = warm[where, :]
        return wide([warmth + energy[where, :], speed[where, :] + lifting_push * warmth])

    def keep(i, ratio, partial, reach):
        where = pl.ds(pl.multiple_of((pl.program_id(0) * rows + i) * layers, layers), layers)
        ratios[where, :] = ratio
        partials[where, :] = partial
        reaches[where, :] = reach

    values = block_sweep(rows, coefficient_at, source_at, span_strength, opens, keep)
    for number, value in enumerate(values):
        for pair in range(PAIRS):
            send[pl.ds(pair * layers * SENT + number, layers, stride=SENT), :] = value[
                :, pair * LANES : (pair + 1) * LANES
            ]


def span_reduced(blocks, received, fluxes):
    values = [received[pl.ds(number, blocks, stride=SENT), :] for number in range(CROSS_SENT)]
    low, high = interface_flux(values, span_strength, blocks)
    fluxes[pl.ds(0, blocks, stride=SIDES), :] = low
    fluxes[pl.ds(1, blocks, stride=SIDES), :] = high


def span_back_cross_forward(
    layers, rows, breadth, warm, flux, ratios, partials, reaches,
    send, chunk_fluxes, cross_ratios, cross_partials, cross_reaches, solved, turned, turned_warm,
):
    halves = breadth // LANES
    lines = layers * rows
    group = min(LANES, lines)
    groups = lines // group
    length = breadth // CHUNKS
    for h in range(halves):
        across = slice(h * LANES, (h + 1) * LANES)
        for g in range(groups):
            turned_warm[g * breadth + h * LANES : g * breadth + (h + 1) * LANES, :] = warm[
                g * group : (g + 1) * group, across
            ].T
    for h in range(halves):
        low, high = (
            wide([
                flux[pl.ds((h * PAIRS + pair) * layers * SIDES + side, layers, stride=SIDES), :]
                for pair in range(PAIRS)
            ])
            for side in range(SIDES)
        )

        def kept_at(i):
            where = slice((h * rows + i) * layers, (h * rows + i + 1) * layers)
            return ratios[where, :], partials[where, :], reaches[where, :]

        def give(i, answer):
            for pair in range(PAIRS):
                start = (h * PAIRS + pair) * lines + i
                solved[pl.ds(start, layers, stride=rows), :] = answer[
                    :, pair * LANES : (pair + 1) * LANES
                ]

        block_return(rows, kept_at, low, high, give)
        for pair in range(PAIRS):
            for g in range(groups):
                start = (h * PAIRS + pair) * lines + g * group
                target = (pair * groups + g) * breadth + h * LANES
                turned[target : target + LANES, :] = solved[start : start + group, :].T

    def chunk_row(ref, number, t):
        return ref[pl.ds(number * breadth + t, CHUNKS, stride=length), :]

    def coefficient_at(t):
        warmth = [chunk_row(turned_warm, g, t) for g in range(groups)]
        return wide([jnp.exp(slope * w) for slope in SLOPES for w in warmth])

    def source_at(t):
        return wide([chunk_row(turned, number, t) for number in range(PAIRS * groups)])

    def keep(t, ratio, partial, reach):
        where = slice(t * CHUNKS, (t + 1) * CHUNKS)
        cross_ratios[where, :] = ratio
        cross_partials[where, :] = partial
        cross_reaches[where, :] = reach

    leading = lax.broadcasted_iota(jnp.int32, (CHUNKS, PAIRS * lines), 0) == 0
    opens = jnp.where(leading, (lax.axis_index("gy") == 0).astype(jnp.float32), 0.0)
    values = block_sweep(length, coefficient_at, source_at, cross_strength, opens, keep)
    linear, merged = merge_chunks(values, cross_strength, CHUNKS)
    for number, value in enumerate(linear):
        chunk_fluxes[number * CHUNKS : (number + 1) * CHUNKS, :] = value
    for number, value in enumerate(merged + merged[-1:]):
        send[number : number + 1, :] = value


def cross_back_depth(
    layers, rows, breadth, parts, warm, *refs
):
    received, refs = refs[:parts], refs[parts:]
    chunk_fluxes, ratios, partials, reaches, new_warmth, new_speed = refs[:6]
    ordered, turned, solved, depth_ratios, depth_partials = refs[6:]
    halves = breadth // LANES
    lines = layers * rows
    group = min(LANES, lines)
    groups = lines // group
    length = breadth // CHUNKS
    own = lax.axis_index("gy")
    for steps in range(parts):
        slot = lax.rem(own + parts - steps, parts)
        ordered[pl.ds(pl.multiple_of(slot * SENT, SENT), SENT), :] = received[steps][...]
    parts_values = [
        [ordered[d * SENT + number : d * SENT + number + 1, :] for number in range(CROSS_SENT)]
        for d in range(parts)
    ]
    end_low, end_high = own_flux(parts_values, cross_strength, own)
    fixed, by_low, by_high = (
        chunk_fluxes[number * CHUNKS : (number + 1) * CHUNKS, :] for number in range(3)
    )
    high = fixed + by_low * end_low + by_high * end_high
    row = lax.broadcasted_iota(jnp.int32, high.shape, 0)
    low = jnp.where(row > 0, pltpu.roll(high, 1, 0), end_low)

    def kept_at(t):
        where = slice(t * CHUNKS, (t + 1) * CHUNKS)
        return ratios[where, :], partials[where, :], reaches[where, :]

    def give(t, answer):
        for number in range(PAIRS * groups):
            turned[pl.ds(number * breadth + t, CHUNKS, stride=length), :] = answer[
                :, number * group : (number + 1) * group
            ]

    block_return(length, kept_at, low, high, give)
    for number in range(PAIRS * groups):
        for h in range(halves):
            start = number * breadth + h * LANES
            solved[number * group : (number + 1) * group, h * LANES : (h + 1) * LANES] = turned[
                start : start + LANES, :
            ].T
    for pair, out in enumerate((new_warmth, new_speed)):
        half = 0.5 * depth_strength

        def coefficient_at(z):
            return jnp.exp(SLOPES[pair] * warm[z * rows : (z + 1) * rows, :])

        def source_at(z):
            return solved[pair * lines + z * rows : pair * lines + (z + 1) * rows, :]

        q_now = coefficient_at(0)
        numerator = source_at(0)
        delta = 1.0 + half * q_now
        for z in range(layers - 1):
            where = slice(z * rows, (z + 1) * rows)
            q_next = coefficient_at(z + 1)
            face = half * (q_now + q_next)
            inverse = 1.0 / (delta + face)
            ratio = face * inverse
            partial = numerator * inverse
            depth_ratios[where, :] = ratio
            depth_partials[where, :] = partial
            delta = 1.0 + delta * ratio
            numerator = source_at(z + 1) + face * partial
            q_now = q_next
        answer = numerator / (delta + half * q_now)
        out[(layers - 1) * rows : layers * rows, :] = answer
        for z in reversed(range(layers - 1)):
            where = slice(z * rows, (z + 1) * rows)
            answer = depth_partials[where, :] + depth_ratios[where, :] * answer
            out[where, :] = answer


def shaped(*shape):
    return jax.ShapeDtypeStruct(shape, jnp.float32)


def held(*shape):
    return pltpu.VMEM(shape, jnp.float32)


def passed(*shape):
    return pltpu.VMEM(shape, jnp.float32)


def near(*values):
    return [pltpu.with_memory_space_constraint(value, pltpu.VMEM) for value in values]


INTERPRET = False


def body(prior_warmth, prior_speed, energy_input):
    layers, rows, breadth = prior_warmth.shape
    lines = layers * rows
    halves = breadth // LANES
    group = min(LANES, lines)
    blocks = lax.axis_size("gx")
    parts = lax.axis_size("gy")
    warm, speed, energy = (v.reshape(lines, breadth) for v in (prior_warmth, prior_speed, energy_input))
    kept = passed(halves * lines, PAIRS * LANES)
    column_spec = pl.BlockSpec((lines, LANES), lambda h: (0, h))
    kept_spec = pl.BlockSpec(memory_space=pltpu.VMEM)
    send_rows = PAIRS * layers * SENT
    send, ratios, partials, reaches = pl.pallas_call(
        functools.partial(span_forward, layers, rows),
        grid=(halves,),
        in_specs=[column_spec] * 3,
        out_specs=(pl.BlockSpec((send_rows, LANES), lambda h: (h, 0)), kept_spec, kept_spec, kept_spec),
        out_shape=(shaped(blocks * SENT, LANES), kept, kept, kept),
        name="span_forward",
        compiler_params=pltpu.CompilerParams(vmem_limit_bytes=ROOM),
        interpret=INTERPRET,
    )(warm, speed, energy)
    received = lax.all_to_all(
        send.reshape(blocks, SENT, LANES), "gx", split_axis=0, concat_axis=0, tiled=True
    )
    flux = pl.pallas_call(
        functools.partial(span_reduced, blocks),
        out_shape=passed(blocks * SIDES, LANES),
        name="span_reduced",
        compiler_params=pltpu.CompilerParams(vmem_limit_bytes=ROOM),
        interpret=INTERPRET,
    )(*near(received.reshape(blocks * SENT, LANES)))
    flux = lax.all_to_all(
        flux.reshape(blocks, SIDES, LANES), "gx", split_axis=0, concat_axis=0, tiled=True
    ).reshape(blocks * SIDES, LANES)
    kept = passed(breadth, PAIRS * lines)
    send, chunk_fluxes, *cross_kept = pl.pallas_call(
        functools.partial(span_back_cross_forward, layers, rows, breadth),
        out_shape=(
            passed(SENT, PAIRS * lines), passed(3 * CHUNKS, PAIRS * lines), kept, kept, kept,
        ),
        scratch_shapes=[
            held(halves * PAIRS * lines, LANES),
            held(PAIRS * lines // group * breadth, group),
            held(lines // group * breadth, group),
        ],
        name="span_back_cross_forward",
        compiler_params=pltpu.CompilerParams(vmem_limit_bytes=ROOM),
        interpret=INTERPRET,
    )(*near(warm, flux, ratios, partials, reaches))
    received = [send] + [
        lax.ppermute(send, "gy", [(i, (i + steps) % parts) for i in range(parts)])
        for steps in range(1, parts)
    ]
    out = shaped(lines, breadth)
    finished = pl.pallas_call(
        functools.partial(cross_back_depth, layers, rows, breadth, parts),
        out_shape=(out, out),
        scratch_shapes=[
            held(parts * SENT, PAIRS * lines),
            held(PAIRS * lines // group * breadth, group),
            held(PAIRS * lines, breadth),
            held(lines, breadth),
            held(lines, breadth),
        ],
        name="cross_back_depth",
        compiler_params=pltpu.CompilerParams(vmem_limit_bytes=ROOM),
        interpret=INTERPRET,
    )(*near(warm, *received, chunk_fluxes, *cross_kept))
    return tuple(v.reshape(layers, rows, breadth) for v in finished)


def solution(mesh):
    in_specs = (P(None, "gx", "gy"), P(None, "gx", "gy"), P(None, "gx", "gy"))
    out_specs = (P(None, "gx", "gy"), P(None, "gx", "gy"))
    return jax.shard_map(body, mesh=mesh, in_specs=in_specs, out_specs=out_specs, check_vma=False)
```

```python
import functools

import jax
import jax.numpy as jnp
from jax import lax
from jax.experimental import pallas as pl
from jax.experimental.pallas import tpu as pltpu
from jax.sharding import PartitionSpec as P

diffusivity_slope = 0.3
stickiness_slope = 0.8
lifting_push = 8.0
span_strength = 1500.0
cross_strength = 1500.0
depth_strength = 2.0

SLOPES = (diffusivity_slope, -stickiness_slope)
PAIRS = 2
LANES = 128
CHUNKS = 8
SENT = 8
SIDES = 2
PIECE = 4
ROOM = 24 * 2**20
CROSS_SENT = 7


def block_sweep(steps, coefficient_at, source_at, strength, opens, keep):
    half = 0.5 * strength
    q_first = q_now = coefficient_at(0)
    numerator = source_at(0)
    delta = 1.0 + opens * (half * q_first)
    weight = jnp.ones_like(q_now)
    first_part = jnp.zeros_like(q_now)
    first_reach = jnp.zeros_like(q_now)
    for step in range(steps):
        if step == steps - 1:
            inverse = 1.0 / delta
            partial = numerator * inverse
            reach = weight * inverse
            keep(step, inverse, partial, reach)
            first_part = first_part + weight * partial
            first_reach = first_reach + weight * reach
            return (first_part, partial, first_reach, reach, inverse, q_first, q_now)
        q_next = coefficient_at(step + 1)
        face = half * (q_now + q_next)
        inverse = 1.0 / (delta + face)
        ratio = face * inverse
        partial = numerator * inverse
        reach = weight * inverse
        keep(step, ratio, partial, reach)
        first_part = first_part + weight * partial
        first_reach = first_reach + weight * reach
        delta = 1.0 + delta * ratio
        weight = weight * ratio
        numerator = source_at(step + 1) + face * partial
        q_now = q_next


def block_return(steps, kept_at, flux_low, flux_high, give):
    answer = None
    for step in reversed(range(steps)):
        ratio, partial, reach = kept_at(step)
        fixed = partial + reach * flux_low
        answer = fixed - ratio * flux_high if answer is None else fixed + ratio * answer
        give(step, answer)


def interface_flux(values, strength, rows):
    first_part, last_part, first_reach, cross_reach, last_reach, q_first, q_last = values
    row = lax.broadcasted_iota(jnp.int32, first_part.shape, 0)

    def following(value):
        return jnp.where(row < rows - 1, pltpu.roll(value, rows - 1, 0), 0.0)

    face = 0.5 * strength * (q_last + following(q_first))
    scale = face / (1.0 + face * (last_reach + following(first_reach)))
    below = jnp.where(row > 0, scale * cross_reach, 0.0)
    above = scale * following(cross_reach)
    flux = scale * (last_part - following(first_part))
    step = 1
    while step < rows:
        below_low, above_low, flux_low = (pltpu.roll(v, step, 0) for v in (below, above, flux))
        below_high, above_high, flux_high = (
            pltpu.roll(v, rows - step, 0) for v in (below, above, flux)
        )
        inverse = 1.0 / (1.0 - below * above_low - above * below_high)
        flux = (flux + below * flux_low + above * flux_high) * inverse
        below = below * below_low * inverse
        above = above * above_high * inverse
        step *= 2
    return jnp.where(row > 0, pltpu.roll(flux, 1, 0), 0.0), flux


def merge_chunks(values, strength, rows):
    first_part, last_part, first_reach, cross_reach, last_reach, q_first, q_last = values
    row = lax.broadcasted_iota(jnp.int32, first_part.shape, 0)

    def following(value):
        return pltpu.roll(value, rows - 1, 0)

    def preceding(value):
        return pltpu.roll(value, 1, 0)

    face = 0.5 * strength * (q_last + following(q_first))
    scale = face / (1.0 + face * (last_reach + following(first_reach)))
    scale = jnp.where(row < rows - 1, scale, 0.0)
    below = scale * cross_reach
    above = scale * following(cross_reach)
    fixed = scale * (last_part - following(first_part))
    by_low = jnp.where(row == 0, below, 0.0)
    by_high = jnp.where(row == rows - 2, above, 0.0)
    below = jnp.where(row > 0, below, 0.0)
    above = jnp.where(row < rows - 2, above, 0.0)
    step = 1
    while step < rows:
        lows = [pltpu.roll(v, step, 0) for v in (below, above, fixed, by_low, by_high)]
        highs = [pltpu.roll(v, rows - step, 0) for v in (below, above, fixed, by_low, by_high)]
        inverse = 1.0 / (1.0 - below * lows[1] - above * highs[0])
        fixed, by_low, by_high = (
            (now + below * low + above * high) * inverse
            for now, low, high in zip((fixed, by_low, by_high), lows[2:], highs[2:])
        )
        below = below * lows[0] * inverse
        above = above * highs[1] * inverse
        step *= 2
    by_high = jnp.where(row < rows - 1, by_high, 1.0)
    merged = (
        (first_part - cross_reach * fixed, 0),
        (last_part + cross_reach * preceding(fixed), rows - 1),
        (first_reach - cross_reach * by_low, 0),
        (cross_reach * preceding(by_low), rows - 1),
        (last_reach - cross_reach * preceding(by_high), rows - 1),
        (q_first, 0),
        (q_last, rows - 1),
    )
    return (fixed, by_low, by_high), [value[at : at + 1, :] for value, at in merged]


def own_flux(parts_values, strength, own):
    half = 0.5 * strength
    ratios, fluxes = [], []
    for j, (_, last_part, _, cross_reach, last_reach, _, q_last) in enumerate(parts_values):
        if j + 1 < len(parts_values):
            first_part, _, first_reach, next_cross, _, q_first, _ = parts_values[j + 1]
            face = half * (q_last + q_first)
            centre = 1.0 + face * (last_reach + first_reach)
            right = face * (last_part - first_part)
            above = face * next_cross
        else:
            face = half * q_last
            centre = 1.0 + face * last_reach
            right = face * last_part
            above = None
        if j:
            below = face * cross_reach
            centre = centre - below * ratios[-1]
            right = right + below * fluxes[-1]
        inverse = 1.0 / centre
        fluxes.append(right * inverse)
        ratios.append(None if above is None else above * inverse)
    high = flux = fluxes[-1]
    low = jnp.zeros_like(flux)
    for j in reversed(range(len(fluxes) - 1)):
        flux = fluxes[j] + ratios[j] * flux
        low = jnp.where(own == j + 1, flux, low)
        high = jnp.where(own == j, flux, high)
    return low, high


def wide(pieces):
    return jnp.concatenate(pieces, axis=1)


def span_forward(
    layers, rows, breadth, warm_far, speed_far, energy_far,
    send, warm, ratios, partials, reaches, speed, energy, arrived,
):
    halves = breadth // LANES
    lines = layers * rows
    opens = (lax.axis_index("gx") == 0).astype(jnp.float32)
    copies = [
        [
            pltpu.make_async_copy(
                far.at[:, h * LANES : (h + 1) * LANES], held_at.at[h * lines : (h + 1) * lines, :], arrived.at[h, k]
            )
            for k, (far, held_at) in enumerate(((warm_far, warm), (energy_far, energy), (speed_far, speed)))
        ]
        for h in range(halves)
    ]
    for some in copies:
        for copy in some:
            copy.start()
    for h in range(halves):
        for copy in copies[h]:
            copy.wait()

        def coefficient_at(i):
            warmth = warm[pl.ds(h * lines + i, layers, stride=rows), :]
            return wide([jnp.exp(slope * warmth) for slope in SLOPES])

        def source_at(i):
            where = pl.ds(h * lines + i, layers, stride=rows)
            warmth = warm[where, :]
            return wide([warmth + energy[where, :], speed[where, :] + lifting_push * warmth])

        def keep(i, ratio, partial, reach):
            where = slice((h * rows + i) * layers, (h * rows + i + 1) * layers)
            ratios[where, :] = ratio
            partials[where, :] = partial
            reaches[where, :] = reach

        values = block_sweep(rows, coefficient_at, source_at, span_strength, opens, keep)
        for number, value in enumerate(values):
            for pair in range(PAIRS):
                start = (h * PAIRS + pair) * layers * SENT + number
                send[pl.ds(start, layers, stride=SENT), :] = value[:, pair * LANES : (pair + 1) * LANES]


def span_reduced(blocks, received, fluxes):
    values = [received[pl.ds(number, blocks, stride=SENT), :] for number in range(CROSS_SENT)]
    low, high = interface_flux(values, span_strength, blocks)
    fluxes[pl.ds(0, blocks, stride=SIDES), :] = low
    fluxes[pl.ds(1, blocks, stride=SIDES), :] = high


def span_back_cross_forward(
    layers, rows, breadth, warm, flux, ratios, partials, reaches,
    send, chunk_fluxes, cross_ratios, cross_partials, cross_reaches, solved, turned, turned_warm,
):
    halves = breadth // LANES
    lines = layers * rows
    group = min(LANES, lines)
    groups = lines // group
    length = breadth // CHUNKS
    for h in range(halves):
        for g in range(groups):
            start = h * lines + g * group
            turned_warm[g * breadth + h * LANES : g * breadth + (h + 1) * LANES, :] = warm[
                start : start + group, :
            ].T
    for h in range(halves):
        low, high = (
            wide([
                flux[pl.ds((h * PAIRS + pair) * layers * SIDES + side, layers, stride=SIDES), :]
                for pair in range(PAIRS)
            ])
            for side in range(SIDES)
        )

        def kept_at(i):
            where = slice((h * rows + i) * layers, (h * rows + i + 1) * layers)
            return ratios[where, :], partials[where, :], reaches[where, :]

        def give(i, answer):
            for pair in range(PAIRS):
                start = (h * PAIRS + pair) * lines + i
                solved[pl.ds(start, layers, stride=rows), :] = answer[
                    :, pair * LANES : (pair + 1) * LANES
                ]

        block_return(rows, kept_at, low, high, give)
        for pair in range(PAIRS):
            for g in range(groups):
                start = (h * PAIRS + pair) * lines + g * group
                target = (pair * groups + g) * breadth + h * LANES
                turned[target : target + LANES, :] = solved[start : start + group, :].T

    def chunk_row(ref, number, t):
        return ref[pl.ds(number * breadth + t, CHUNKS, stride=length), :]

    def coefficient_at(t):
        warmth = [chunk_row(turned_warm, g, t) for g in range(groups)]
        return wide([jnp.exp(slope * w) for slope in SLOPES for w in warmth])

    def source_at(t):
        return wide([chunk_row(turned, number, t) for number in range(PAIRS * groups)])

    def keep(t, ratio, partial, reach):
        where = slice(t * CHUNKS, (t + 1) * CHUNKS)
        cross_ratios[where, :] = ratio
        cross_partials[where, :] = partial
        cross_reaches[where, :] = reach

    leading = lax.broadcasted_iota(jnp.int32, (CHUNKS, PAIRS * lines), 0) == 0
    opens = jnp.where(leading, (lax.axis_index("gy") == 0).astype(jnp.float32), 0.0)
    values = block_sweep(length, coefficient_at, source_at, cross_strength, opens, keep)
    linear, merged = merge_chunks(values, cross_strength, CHUNKS)
    for number, value in enumerate(linear):
        chunk_fluxes[number * CHUNKS : (number + 1) * CHUNKS, :] = value
    for number, value in enumerate(merged + merged[-1:]):
        send[number : number + 1, :] = value


def cross_back_depth(
    layers, rows, breadth, parts, warm, *refs
):
    received, refs = refs[:parts], refs[parts:]
    chunk_fluxes, ratios, partials, reaches, new_warmth, new_speed = refs[:6]
    ordered, turned, solved, depth_ratios, depth_partials, *finished = refs[6:]
    left = finished.pop()
    copies = []
    halves = breadth // LANES
    lines = layers * rows
    group = min(LANES, lines)
    groups = lines // group
    length = breadth // CHUNKS
    own = lax.axis_index("gy")
    for steps in range(parts):
        slot = lax.rem(own + parts - steps, parts)
        ordered[pl.ds(pl.multiple_of(slot * SENT, SENT), SENT), :] = received[steps][...]
    parts_values = [
        [ordered[d * SENT + number : d * SENT + number + 1, :] for number in range(CROSS_SENT)]
        for d in range(parts)
    ]
    end_low, end_high = own_flux(parts_values, cross_strength, own)
    fixed, by_low, by_high = (
        chunk_fluxes[number * CHUNKS : (number + 1) * CHUNKS, :] for number in range(3)
    )
    high = fixed + by_low * end_low + by_high * end_high
    row = lax.broadcasted_iota(jnp.int32, high.shape, 0)
    low = jnp.where(row > 0, pltpu.roll(high, 1, 0), end_low)

    def kept_at(t):
        where = slice(t * CHUNKS, (t + 1) * CHUNKS)
        return ratios[where, :], partials[where, :], reaches[where, :]

    def give(t, answer):
        for number in range(PAIRS * groups):
            turned[pl.ds(number * breadth + t, CHUNKS, stride=length), :] = answer[
                :, number * group : (number + 1) * group
            ]

    block_return(length, kept_at, low, high, give)
    for number in range(PAIRS * groups):
        for h in range(halves):
            start = number * breadth + h * LANES
            solved[number * group : (number + 1) * group, h * LANES : (h + 1) * LANES] = turned[
                start : start + LANES, :
            ].T
    for pair, (far, out) in enumerate(zip((new_warmth, new_speed), finished)):
        half = 0.5 * depth_strength

        def coefficient_at(z):
            starts = [h * lines + z * rows for h in range(halves)]
            return jnp.exp(SLOPES[pair] * wide([warm[start : start + rows, :] for start in starts]))

        def source_at(z):
            return solved[pair * lines + z * rows : pair * lines + (z + 1) * rows, :]

        q_now = coefficient_at(0)
        numerator = source_at(0)
        delta = 1.0 + half * q_now
        for z in range(layers - 1):
            where = slice(z * rows, (z + 1) * rows)
            q_next = coefficient_at(z + 1)
            face = half * (q_now + q_next)
            inverse = 1.0 / (delta + face)
            ratio = face * inverse
            partial = numerator * inverse
            depth_ratios[where, :] = ratio
            depth_partials[where, :] = partial
            delta = 1.0 + delta * ratio
            numerator = source_at(z + 1) + face * partial
            q_now = q_next
        answer = numerator / (delta + half * q_now)
        out[(layers - 1) * rows : layers * rows, :] = answer
        for z in reversed(range(layers - 1)):
            where = slice(z * rows, (z + 1) * rows)
            answer = depth_partials[where, :] + depth_ratios[where, :] * answer
            out[where, :] = answer
            if z % PIECE == 0:
                piece = pl.ds(z * rows, PIECE * rows)
                copies.append(
                    pltpu.make_async_copy(out.at[piece, :], far.at[piece, :], left.at[pair, z // PIECE])
                )
                copies[-1].start()
    for copy in copies:
        copy.wait()


def shaped(*shape):
    return jax.ShapeDtypeStruct(shape, jnp.float32)


def held(*shape):
    return pltpu.VMEM(shape, jnp.float32)


def passed(*shape):
    return pltpu.VMEM(shape, jnp.float32)


def distant(*values):
    return [pltpu.with_memory_space_constraint(value, pltpu.HBM) for value in values]


def near(*values):
    return [pltpu.with_memory_space_constraint(value, pltpu.VMEM) for value in values]


INTERPRET = False


def body(prior_warmth, prior_speed, energy_input):
    layers, rows, breadth = prior_warmth.shape
    lines = layers * rows
    halves = breadth // LANES
    group = min(LANES, lines)
    blocks = lax.axis_size("gx")
    parts = lax.axis_size("gy")
    warm, speed, energy = (v.reshape(lines, breadth) for v in (prior_warmth, prior_speed, energy_input))
    kept = passed(halves * lines, PAIRS * LANES)
    column = (halves * lines, LANES)
    far = pl.BlockSpec(memory_space=pltpu.HBM)
    send, warm, ratios, partials, reaches = pl.pallas_call(
        functools.partial(span_forward, layers, rows, breadth),
        in_specs=[far] * 3,
        out_shape=(passed(blocks * SENT, LANES), passed(*column), kept, kept, kept),
        scratch_shapes=[held(*column), held(*column), pltpu.SemaphoreType.DMA((halves, 3))],
        name="span_forward",
        compiler_params=pltpu.CompilerParams(vmem_limit_bytes=ROOM),
        interpret=INTERPRET,
    )(*distant(warm, speed, energy))
    received = lax.all_to_all(
        send.reshape(blocks, SENT, LANES), "gx", split_axis=0, concat_axis=0, tiled=True
    )
    flux = pl.pallas_call(
        functools.partial(span_reduced, blocks),
        out_shape=passed(blocks * SIDES, LANES),
        name="span_reduced",
        compiler_params=pltpu.CompilerParams(vmem_limit_bytes=ROOM),
        interpret=INTERPRET,
    )(*near(received.reshape(blocks * SENT, LANES)))
    flux = lax.all_to_all(
        flux.reshape(blocks, SIDES, LANES), "gx", split_axis=0, concat_axis=0, tiled=True
    ).reshape(blocks * SIDES, LANES)
    kept = passed(breadth, PAIRS * lines)
    send, chunk_fluxes, *cross_kept = pl.pallas_call(
        functools.partial(span_back_cross_forward, layers, rows, breadth),
        out_shape=(
            passed(SENT, PAIRS * lines), passed(3 * CHUNKS, PAIRS * lines), kept, kept, kept,
        ),
        scratch_shapes=[
            held(halves * PAIRS * lines, LANES),
            held(PAIRS * lines // group * breadth, group),
            held(lines // group * breadth, group),
        ],
        name="span_back_cross_forward",
        compiler_params=pltpu.CompilerParams(vmem_limit_bytes=ROOM),
        interpret=INTERPRET,
    )(*near(warm, flux, ratios, partials, reaches))
    received = [send] + [
        lax.ppermute(send, "gy", [(i, (i + steps) % parts) for i in range(parts)])
        for steps in range(1, parts)
    ]
    out = shaped(lines, breadth)
    finished = pl.pallas_call(
        functools.partial(cross_back_depth, layers, rows, breadth, parts),
        out_shape=(out, out),
        out_specs=(far, far),
        scratch_shapes=[
            held(parts * SENT, PAIRS * lines),
            held(PAIRS * lines // group * breadth, group),
            held(PAIRS * lines, breadth),
            held(lines, breadth),
            held(lines, breadth),
            held(lines, breadth),
            held(lines, breadth),
            pltpu.SemaphoreType.DMA((PAIRS, layers // PIECE)),
        ],
        name="cross_back_depth",
        compiler_params=pltpu.CompilerParams(vmem_limit_bytes=ROOM),
        interpret=INTERPRET,
    )(*near(warm, *received, chunk_fluxes, *cross_kept))
    return tuple(v.reshape(layers, rows, breadth) for v in finished)


def solution(mesh):
    in_specs = (P(None, "gx", "gy"), P(None, "gx", "gy"), P(None, "gx", "gy"))
    out_specs = (P(None, "gx", "gy"), P(None, "gx", "gy"))
    return jax.shard_map(body, mesh=mesh, in_specs=in_specs, out_specs=out_specs, check_vma=False)
```

```python
import functools

import jax
import jax.numpy as jnp
from jax import lax
from jax.experimental import pallas as pl
from jax.experimental.pallas import tpu as pltpu
from jax.sharding import PartitionSpec as P

diffusivity_slope = 0.3
stickiness_slope = 0.8
lifting_push = 8.0
span_strength = 1500.0
cross_strength = 1500.0
depth_strength = 2.0

SLOPES = (diffusivity_slope, -stickiness_slope)
PAIRS = 2
LANES = 128
CHUNKS = 8
SENT = 8
SIDES = 2
SPAN_SENT = 6
PIECE = 4
ROOM = 24 * 2**20
CROSS_SENT = 7


def block_sweep(steps, coefficient_at, source_at, strength, opens, keep):
    half = 0.5 * strength
    q_first = q_now = coefficient_at(0)
    numerator = source_at(0)
    delta = 1.0 + opens * (half * q_first)
    weight = jnp.ones_like(q_now)
    first_part = jnp.zeros_like(q_now)
    first_reach = jnp.zeros_like(q_now)
    for step in range(steps):
        if step == steps - 1:
            inverse = 1.0 / delta
            partial = numerator * inverse
            reach = weight * inverse
            keep(step, inverse, partial, reach)
            first_part = first_part + weight * partial
            first_reach = first_reach + weight * reach
            return (first_part, partial, first_reach, reach, inverse, q_first, q_now)
        q_next = coefficient_at(step + 1)
        face = half * (q_now + q_next)
        inverse = 1.0 / (delta + face)
        ratio = face * inverse
        partial = numerator * inverse
        reach = weight * inverse
        keep(step, ratio, partial, reach)
        first_part = first_part + weight * partial
        first_reach = first_reach + weight * reach
        delta = 1.0 + delta * ratio
        weight = weight * ratio
        numerator = source_at(step + 1) + face * partial
        q_now = q_next


def block_return(steps, kept_at, flux_low, flux_high, give):
    answer = None
    for step in reversed(range(steps)):
        ratio, partial, reach = kept_at(step)
        fixed = partial + reach * flux_low
        answer = fixed - ratio * flux_high if answer is None else fixed + ratio * answer
        give(step, answer)


def interface_flux(values, strength, rows):
    first_part, last_part, first_reach, cross_reach, last_reach, q_first, q_last = values
    row = lax.broadcasted_iota(jnp.int32, first_part.shape, 0)

    def following(value):
        return jnp.where(row < rows - 1, pltpu.roll(value, rows - 1, 0), 0.0)

    face = 0.5 * strength * (q_last + following(q_first))
    scale = face / (1.0 + face * (last_reach + following(first_reach)))
    below = jnp.where(row > 0, scale * cross_reach, 0.0)
    above = scale * following(cross_reach)
    flux = scale * (last_part - following(first_part))
    step = 1
    while step < rows:
        below_low, above_low, flux_low = (pltpu.roll(v, step, 0) for v in (below, above, flux))
        below_high, above_high, flux_high = (
            pltpu.roll(v, rows - step, 0) for v in (below, above, flux)
        )
        inverse = 1.0 / (1.0 - below * above_low - above * below_high)
        flux = (flux + below * flux_low + above * flux_high) * inverse
        below = below * below_low * inverse
        above = above * above_high * inverse
        step *= 2
    return jnp.where(row > 0, pltpu.roll(flux, 1, 0), 0.0), flux


def merge_chunks(values, strength, rows):
    first_part, last_part, first_reach, cross_reach, last_reach, q_first, q_last = values
    row = lax.broadcasted_iota(jnp.int32, first_part.shape, 0)

    def following(value):
        return pltpu.roll(value, rows - 1, 0)

    def preceding(value):
        return pltpu.roll(value, 1, 0)

    face = 0.5 * strength * (q_last + following(q_first))
    scale = face / (1.0 + face * (last_reach + following(first_reach)))
    scale = jnp.where(row < rows - 1, scale, 0.0)
    below = scale * cross_reach
    above = scale * following(cross_reach)
    fixed = scale * (last_part - following(first_part))
    by_low = jnp.where(row == 0, below, 0.0)
    by_high = jnp.where(row == rows - 2, above, 0.0)
    below = jnp.where(row > 0, below, 0.0)
    above = jnp.where(row < rows - 2, above, 0.0)
    step = 1
    while step < rows:
        lows = [pltpu.roll(v, step, 0) for v in (below, above, fixed, by_low, by_high)]
        highs = [pltpu.roll(v, rows - step, 0) for v in (below, above, fixed, by_low, by_high)]
        inverse = 1.0 / (1.0 - below * lows[1] - above * highs[0])
        fixed, by_low, by_high = (
            (now + below * low + above * high) * inverse
            for now, low, high in zip((fixed, by_low, by_high), lows[2:], highs[2:])
        )
        below = below * lows[0] * inverse
        above = above * highs[1] * inverse
        step *= 2
    by_high = jnp.where(row < rows - 1, by_high, 1.0)
    merged = (
        (first_part - cross_reach * fixed, 0),
        (last_part + cross_reach * preceding(fixed), rows - 1),
        (first_reach - cross_reach * by_low, 0),
        (cross_reach * preceding(by_low), rows - 1),
        (last_reach - cross_reach * preceding(by_high), rows - 1),
        (q_first, 0),
        (q_last, rows - 1),
    )
    return (fixed, by_low, by_high), [value[at : at + 1, :] for value, at in merged]


def own_flux(parts_values, strength, own):
    half = 0.5 * strength
    ratios, fluxes = [], []
    for j, (_, last_part, _, cross_reach, last_reach, _, q_last) in enumerate(parts_values):
        if j + 1 < len(parts_values):
            first_part, _, first_reach, next_cross, _, q_first, _ = parts_values[j + 1]
            face = half * (q_last + q_first)
            centre = 1.0 + face * (last_reach + first_reach)
            right = face * (last_part - first_part)
            above = face * next_cross
        else:
            face = half * q_last
            centre = 1.0 + face * last_reach
            right = face * last_part
            above = None
        if j:
            below = face * cross_reach
            centre = centre - below * ratios[-1]
            right = right + below * fluxes[-1]
        inverse = 1.0 / centre
        fluxes.append(right * inverse)
        ratios.append(None if above is None else above * inverse)
    high = flux = fluxes[-1]
    low = jnp.zeros_like(flux)
    for j in reversed(range(len(fluxes) - 1)):
        flux = fluxes[j] + ratios[j] * flux
        low = jnp.where(own == j + 1, flux, low)
        high = jnp.where(own == j, flux, high)
    return low, high


def left_half(like):
    return lax.broadcasted_iota(jnp.int32, like.shape, 1) < LANES // 2


def cross_halves(one, other):
    left = left_half(one)
    return (
        jnp.where(left, one, pltpu.roll(other, LANES // 2, 1)),
        jnp.where(left, pltpu.roll(one, LANES // 2, 1), other),
    )


def wide(pieces):
    return jnp.concatenate(pieces, axis=1)


def span_forward(
    layers, rows, breadth, warm_far, speed_far, energy_far,
    send, warm, ratios, partials, reaches, speed, energy, arrived,
):
    halves = breadth // LANES
    lines = layers * rows
    opens = (lax.axis_index("gx") == 0).astype(jnp.float32)
    copies = [
        [
            pltpu.make_async_copy(
                far.at[:, h * LANES : (h + 1) * LANES], held_at.at[h * lines : (h + 1) * lines, :], arrived.at[h, k]
            )
            for k, (far, held_at) in enumerate(((warm_far, warm), (energy_far, energy), (speed_far, speed)))
        ]
        for h in range(halves)
    ]
    for some in copies:
        for copy in some:
            copy.start()
    for h in range(halves):
        for copy in copies[h]:
            copy.wait()

        def coefficient_at(i):
            warmth = warm[pl.ds(h * lines + i, layers, stride=rows), :]
            return wide([jnp.exp(slope * warmth) for slope in SLOPES])

        def source_at(i):
            where = pl.ds(h * lines + i, layers, stride=rows)
            warmth = warm[where, :]
            return wide([warmth + energy[where, :], speed[where, :] + lifting_push * warmth])

        def keep(i, ratio, partial, reach):
            where = slice((h * rows + i) * layers, (h * rows + i + 1) * layers)
            ratios[where, :] = ratio
            partials[where, :] = partial
            reaches[where, :] = reach

        values = block_sweep(rows, coefficient_at, source_at, span_strength, opens, keep)[:5]
        sides = [(value[:, :LANES], value[:, LANES:]) for value in values]
        sides.append(tuple(warm[pl.ds(h * lines + i, layers, stride=rows), :] for i in (0, rows - 1)))
        for number, (one, other) in enumerate(sides):
            for part, value in enumerate(cross_halves(one, other)):
                start = (h * PAIRS + part) * layers * SPAN_SENT + number
                send[pl.ds(start, layers, stride=SPAN_SENT), :] = value


def span_reduced(blocks, received, fluxes):
    values = [received[pl.ds(number, blocks, stride=SPAN_SENT), :] for number in range(SPAN_SENT)]
    edges = values.pop()
    left = left_half(edges)
    turned = pltpu.roll(edges, LANES // 2, 1)
    slope = jnp.where(left, SLOPES[0], SLOPES[1])
    values += [jnp.exp(slope * jnp.where(left, one, other)) for one, other in ((edges, turned), (turned, edges))]
    low, high = interface_flux(values, span_strength, blocks)
    fluxes[pl.ds(0, blocks, stride=SIDES), :] = low
    fluxes[pl.ds(1, blocks, stride=SIDES), :] = high


def span_back_cross_forward(
    layers, rows, breadth, warm, flux, ratios, partials, reaches,
    send, chunk_fluxes, cross_ratios, cross_partials, cross_reaches, solved, turned, turned_warm,
):
    halves = breadth // LANES
    lines = layers * rows
    group = min(LANES, lines)
    groups = lines // group
    length = breadth // CHUNKS
    for h in range(halves):
        for g in range(groups):
            start = h * lines + g * group
            turned_warm[g * breadth + h * LANES : g * breadth + (h + 1) * LANES, :] = warm[
                start : start + group, :
            ].T
    for h in range(halves):
        low, high = (
            wide(cross_halves(*(
                flux[pl.ds((h * PAIRS + part) * layers * SIDES + side, layers, stride=SIDES), :]
                for part in range(PAIRS)
            )))
            for side in range(SIDES)
        )

        def kept_at(i):
            where = slice((h * rows + i) * layers, (h * rows + i + 1) * layers)
            return ratios[where, :], partials[where, :], reaches[where, :]

        def give(i, answer):
            for pair in range(PAIRS):
                start = (h * PAIRS + pair) * lines + i
                solved[pl.ds(start, layers, stride=rows), :] = answer[
                    :, pair * LANES : (pair + 1) * LANES
                ]

        block_return(rows, kept_at, low, high, give)
        for pair in range(PAIRS):
            for g in range(groups):
                start = (h * PAIRS + pair) * lines + g * group
                target = (pair * groups + g) * breadth + h * LANES
                turned[target : target + LANES, :] = solved[start : start + group, :].T

    def chunk_row(ref, number, t):
        return ref[pl.ds(number * breadth + t, CHUNKS, stride=length), :]

    def coefficient_at(t):
        warmth = [chunk_row(turned_warm, g, t) for g in range(groups)]
        return wide([jnp.exp(slope * w) for slope in SLOPES for w in warmth])

    def source_at(t):
        return wide([chunk_row(turned, number, t) for number in range(PAIRS * groups)])

    def keep(t, ratio, partial, reach):
        where = slice(t * CHUNKS, (t + 1) * CHUNKS)
        cross_ratios[where, :] = ratio
        cross_partials[where, :] = partial
        cross_reaches[where, :] = reach

    leading = lax.broadcasted_iota(jnp.int32, (CHUNKS, PAIRS * lines), 0) == 0
    opens = jnp.where(leading, (lax.axis_index("gy") == 0).astype(jnp.float32), 0.0)
    values = block_sweep(length, coefficient_at, source_at, cross_strength, opens, keep)
    linear, merged = merge_chunks(values, cross_strength, CHUNKS)
    for number, value in enumerate(linear):
        chunk_fluxes[number * CHUNKS : (number + 1) * CHUNKS, :] = value
    for number, value in enumerate(merged + merged[-1:]):
        send[number : number + 1, :] = value


def cross_back_depth(
    layers, rows, breadth, parts, warm, *refs
):
    received, refs = refs[:parts], refs[parts:]
    chunk_fluxes, ratios, partials, reaches, new_warmth, new_speed = refs[:6]
    ordered, turned, solved, depth_ratios, depth_partials, *finished = refs[6:]
    left = finished.pop()
    copies = []
    halves = breadth // LANES
    lines = layers * rows
    group = min(LANES, lines)
    groups = lines // group
    length = breadth // CHUNKS
    own = lax.axis_index("gy")
    for number, steps in enumerate(by_distance(parts)):
        slot = lax.rem(own + parts - steps, parts)
        ordered[pl.ds(pl.multiple_of(slot * SENT, SENT), SENT), :] = received[number][...]
    parts_values = [
        [ordered[d * SENT + number : d * SENT + number + 1, :] for number in range(CROSS_SENT)]
        for d in range(parts)
    ]
    end_low, end_high = own_flux(parts_values, cross_strength, own)
    fixed, by_low, by_high = (
        chunk_fluxes[number * CHUNKS : (number + 1) * CHUNKS, :] for number in range(3)
    )
    high = fixed + by_low * end_low + by_high * end_high
    row = lax.broadcasted_iota(jnp.int32, high.shape, 0)
    low = jnp.where(row > 0, pltpu.roll(high, 1, 0), end_low)

    def kept_at(t):
        where = slice(t * CHUNKS, (t + 1) * CHUNKS)
        return ratios[where, :], partials[where, :], reaches[where, :]

    def give(t, answer):
        for number in range(PAIRS * groups):
            turned[pl.ds(number * breadth + t, CHUNKS, stride=length), :] = answer[
                :, number * group : (number + 1) * group
            ]

    block_return(length, kept_at, low, high, give)
    for number in range(PAIRS * groups):
        for h in range(halves):
            start = number * breadth + h * LANES
            solved[number * group : (number + 1) * group, h * LANES : (h + 1) * LANES] = turned[
                start : start + LANES, :
            ].T
    for pair, (far, out) in enumerate(zip((new_warmth, new_speed), finished)):
        half = 0.5 * depth_strength

        def coefficient_at(z):
            starts = [h * lines + z * rows for h in range(halves)]
            return jnp.exp(SLOPES[pair] * wide([warm[start : start + rows, :] for start in starts]))

        def source_at(z):
            return solved[pair * lines + z * rows : pair * lines + (z + 1) * rows, :]

        q_now = coefficient_at(0)
        numerator = source_at(0)
        delta = 1.0 + half * q_now
        for z in range(layers - 1):
            where = slice(z * rows, (z + 1) * rows)
            q_next = coefficient_at(z + 1)
            face = half * (q_now + q_next)
            inverse = 1.0 / (delta + face)
            ratio = face * inverse
            partial = numerator * inverse
            depth_ratios[where, :] = ratio
            depth_partials[where, :] = partial
            delta = 1.0 + delta * ratio
            numerator = source_at(z + 1) + face * partial
            q_now = q_next
        answer = numerator / (delta + half * q_now)
        out[(layers - 1) * rows : layers * rows, :] = answer
        for z in reversed(range(layers - 1)):
            where = slice(z * rows, (z + 1) * rows)
            answer = depth_partials[where, :] + depth_ratios[where, :] * answer
            out[where, :] = answer
            if z % PIECE == 0:
                piece = pl.ds(z * rows, PIECE * rows)
                copies.append(
                    pltpu.make_async_copy(out.at[piece, :], far.at[piece, :], left.at[pair, z // PIECE])
                )
                copies[-1].start()
    for copy in copies:
        copy.wait()


def by_distance(parts):
    return sorted(range(parts), key=lambda steps: min(steps, parts - steps))


def shaped(*shape):
    return jax.ShapeDtypeStruct(shape, jnp.float32)


def held(*shape):
    return pltpu.VMEM(shape, jnp.float32)


def passed(*shape):
    return pltpu.VMEM(shape, jnp.float32)


def distant(*values):
    return [pltpu.with_memory_space_constraint(value, pltpu.HBM) for value in values]


def near(*values):
    return [pltpu.with_memory_space_constraint(value, pltpu.VMEM) for value in values]


INTERPRET = False


def body(prior_warmth, prior_speed, energy_input):
    layers, rows, breadth = prior_warmth.shape
    lines = layers * rows
    halves = breadth // LANES
    group = min(LANES, lines)
    blocks = lax.axis_size("gx")
    parts = lax.axis_size("gy")
    warm, speed, energy = (v.reshape(lines, breadth) for v in (prior_warmth, prior_speed, energy_input))
    kept = passed(halves * lines, PAIRS * LANES)
    column = (halves * lines, LANES)
    far = pl.BlockSpec(memory_space=pltpu.HBM)
    send, warm, ratios, partials, reaches = pl.pallas_call(
        functools.partial(span_forward, layers, rows, breadth),
        in_specs=[far] * 3,
        out_shape=(passed(blocks * SPAN_SENT, LANES), passed(*column), kept, kept, kept),
        scratch_shapes=[held(*column), held(*column), pltpu.SemaphoreType.DMA((halves, 3))],
        name="span_forward",
        compiler_params=pltpu.CompilerParams(vmem_limit_bytes=ROOM),
        interpret=INTERPRET,
    )(*distant(warm, speed, energy))
    received = lax.all_to_all(
        send.reshape(-1, SIDES, LANES), "gx", split_axis=0, concat_axis=0, tiled=True
    )
    flux = pl.pallas_call(
        functools.partial(span_reduced, blocks),
        out_shape=passed(blocks * SIDES, LANES),
        name="span_reduced",
        compiler_params=pltpu.CompilerParams(vmem_limit_bytes=ROOM),
        interpret=INTERPRET,
    )(*near(received.reshape(blocks * SPAN_SENT, LANES)))
    flux = lax.all_to_all(
        flux.reshape(blocks, SIDES, LANES), "gx", split_axis=0, concat_axis=0, tiled=True
    ).reshape(blocks * SIDES, LANES)
    kept = passed(breadth, PAIRS * lines)
    send, chunk_fluxes, *cross_kept = pl.pallas_call(
        functools.partial(span_back_cross_forward, layers, rows, breadth),
        out_shape=(
            passed(SENT, PAIRS * lines), passed(3 * CHUNKS, PAIRS * lines), kept, kept, kept,
        ),
        scratch_shapes=[
            held(halves * PAIRS * lines, LANES),
            held(PAIRS * lines // group * breadth, group),
            held(lines // group * breadth, group),
        ],
        name="span_back_cross_forward",
        compiler_params=pltpu.CompilerParams(vmem_limit_bytes=ROOM),
        interpret=INTERPRET,
    )(*near(warm, flux, ratios, partials, reaches))
    received = [
        lax.ppermute(send, "gy", [(i, (i + steps) % parts) for i in range(parts)]) if steps else send
        for steps in by_distance(parts)
    ]
    out = shaped(lines, breadth)
    finished = pl.pallas_call(
        functools.partial(cross_back_depth, layers, rows, breadth, parts),
        out_shape=(out, out),
        out_specs=(far, far),
        scratch_shapes=[
            held(parts * SENT, PAIRS * lines),
            held(PAIRS * lines // group * breadth, group),
            held(PAIRS * lines, breadth),
            held(lines, breadth),
            held(lines, breadth),
            held(lines, breadth),
            held(lines, breadth),
            pltpu.SemaphoreType.DMA((PAIRS, layers // PIECE)),
        ],
        name="cross_back_depth",
        compiler_params=pltpu.CompilerParams(vmem_limit_bytes=ROOM),
        interpret=INTERPRET,
    )(*near(warm, *received, chunk_fluxes, *cross_kept))
    return tuple(v.reshape(layers, rows, breadth) for v in finished)


def solution(mesh):
    in_specs = (P(None, "gx", "gy"), P(None, "gx", "gy"), P(None, "gx", "gy"))
    out_specs = (P(None, "gx", "gy"), P(None, "gx", "gy"))
    return jax.shard_map(body, mesh=mesh, in_specs=in_specs, out_specs=out_specs, check_vma=False)
```

```python
import functools

import jax
import jax.numpy as jnp
from jax import lax
from jax.experimental import pallas as pl
from jax.experimental.pallas import tpu as pltpu
from jax.sharding import PartitionSpec as P

diffusivity_slope = 0.3
stickiness_slope = 0.8
lifting_push = 8.0
span_strength = 1500.0
cross_strength = 1500.0
depth_strength = 2.0

SLOPES = (diffusivity_slope, -stickiness_slope)
PAIRS = 2
LANES = 128
CHUNKS = 8
SENT = 8
SIDES = 2
TRADED = 3
SPAN_SENT = 6
PIECE = 4
ROOM = 24 * 2**20
CROSS_SENT = 7


def block_sweep(steps, coefficient_at, source_at, strength, opens, keep):
    half = 0.5 * strength
    q_first = q_now = coefficient_at(0)
    numerator = source_at(0)
    delta = 1.0 + opens * (half * q_first)
    weight = jnp.ones_like(q_now)
    first_part = jnp.zeros_like(q_now)
    first_reach = jnp.zeros_like(q_now)
    for step in range(steps):
        if step == steps - 1:
            inverse = 1.0 / delta
            partial = numerator * inverse
            reach = weight * inverse
            keep(step, inverse, partial, reach)
            first_part = first_part + weight * partial
            first_reach = first_reach + weight * reach
            return (first_part, partial, first_reach, reach, inverse, q_first, q_now)
        q_next = coefficient_at(step + 1)
        face = half * (q_now + q_next)
        inverse = 1.0 / (delta + face)
        ratio = face * inverse
        partial = numerator * inverse
        reach = weight * inverse
        keep(step, ratio, partial, reach)
        first_part = first_part + weight * partial
        first_reach = first_reach + weight * reach
        delta = 1.0 + delta * ratio
        weight = weight * ratio
        numerator = source_at(step + 1) + face * partial
        q_now = q_next


def block_return(steps, kept_at, flux_low, flux_high, give):
    answer = None
    for step in reversed(range(steps)):
        ratio, partial, reach = kept_at(step)
        fixed = partial + reach * flux_low
        answer = fixed - ratio * flux_high if answer is None else fixed + ratio * answer
        give(step, answer)


def interface_flux(values, strength, rows):
    first_part, last_part, first_reach, cross_reach, last_reach, q_first, q_last = values
    row = lax.broadcasted_iota(jnp.int32, first_part.shape, 0)

    def following(value):
        return jnp.where(row < rows - 1, pltpu.roll(value, rows - 1, 0), 0.0)

    face = 0.5 * strength * (q_last + following(q_first))
    scale = face / (1.0 + face * (last_reach + following(first_reach)))
    below = jnp.where(row > 0, scale * cross_reach, 0.0)
    above = scale * following(cross_reach)
    flux = scale * (last_part - following(first_part))
    step = 1
    while step < rows:
        below_low, above_low, flux_low = (pltpu.roll(v, step, 0) for v in (below, above, flux))
        below_high, above_high, flux_high = (
            pltpu.roll(v, rows - step, 0) for v in (below, above, flux)
        )
        inverse = 1.0 / (1.0 - below * above_low - above * below_high)
        flux = (flux + below * flux_low + above * flux_high) * inverse
        below = below * below_low * inverse
        above = above * above_high * inverse
        step *= 2
    return jnp.where(row > 0, pltpu.roll(flux, 1, 0), 0.0), flux


def merge_chunks(values, strength, rows):
    first_part, last_part, first_reach, cross_reach, last_reach, q_first, q_last = values
    row = lax.broadcasted_iota(jnp.int32, first_part.shape, 0)

    def following(value):
        return pltpu.roll(value, rows - 1, 0)

    def preceding(value):
        return pltpu.roll(value, 1, 0)

    face = 0.5 * strength * (q_last + following(q_first))
    scale = face / (1.0 + face * (last_reach + following(first_reach)))
    scale = jnp.where(row < rows - 1, scale, 0.0)
    below = scale * cross_reach
    above = scale * following(cross_reach)
    fixed = scale * (last_part - following(first_part))
    by_low = jnp.where(row == 0, below, 0.0)
    by_high = jnp.where(row == rows - 2, above, 0.0)
    below = jnp.where(row > 0, below, 0.0)
    above = jnp.where(row < rows - 2, above, 0.0)
    step = 1
    while step < rows:
        lows = [pltpu.roll(v, step, 0) for v in (below, above, fixed, by_low, by_high)]
        highs = [pltpu.roll(v, rows - step, 0) for v in (below, above, fixed, by_low, by_high)]
        inverse = 1.0 / (1.0 - below * lows[1] - above * highs[0])
        fixed, by_low, by_high = (
            (now + below * low + above * high) * inverse
            for now, low, high in zip((fixed, by_low, by_high), lows[2:], highs[2:])
        )
        below = below * lows[0] * inverse
        above = above * highs[1] * inverse
        step *= 2
    by_high = jnp.where(row < rows - 1, by_high, 1.0)
    merged = (
        (first_part - cross_reach * fixed, 0),
        (last_part + cross_reach * preceding(fixed), rows - 1),
        (first_reach - cross_reach * by_low, 0),
        (cross_reach * preceding(by_low), rows - 1),
        (last_reach - cross_reach * preceding(by_high), rows - 1),
        (q_first, 0),
        (q_last, rows - 1),
    )
    return (fixed, by_low, by_high), [value[at : at + 1, :] for value, at in merged]


def own_flux(parts_values, strength, own):
    half = 0.5 * strength
    ratios, fluxes = [], []
    for j, (_, last_part, _, cross_reach, last_reach, _, q_last) in enumerate(parts_values):
        if j + 1 < len(parts_values):
            first_part, _, first_reach, next_cross, _, q_first, _ = parts_values[j + 1]
            face = half * (q_last + q_first)
            centre = 1.0 + face * (last_reach + first_reach)
            right = face * (last_part - first_part)
            above = face * next_cross
        else:
            face = half * q_last
            centre = 1.0 + face * last_reach
            right = face * last_part
            above = None
        if j:
            below = face * cross_reach
            centre = centre - below * ratios[-1]
            right = right + below * fluxes[-1]
        inverse = 1.0 / centre
        fluxes.append(right * inverse)
        ratios.append(None if above is None else above * inverse)
    high = flux = fluxes[-1]
    low = jnp.zeros_like(flux)
    for j in reversed(range(len(fluxes) - 1)):
        flux = fluxes[j] + ratios[j] * flux
        low = jnp.where(own == j + 1, flux, low)
        high = jnp.where(own == j, flux, high)
    return low, high


def left_half(like):
    return lax.broadcasted_iota(jnp.int32, like.shape, 1) < LANES // 2


def cross_halves(one, other):
    left = left_half(one)
    return (
        jnp.where(left, one, pltpu.roll(other, LANES // 2, 1)),
        jnp.where(left, pltpu.roll(one, LANES // 2, 1), other),
    )


def wide(pieces):
    return jnp.concatenate(pieces, axis=1)


def span_forward(
    layers, rows, breadth, warm_far, speed_far, energy_far,
    send, warm, ratios, partials, reaches, speed, energy, arrived,
):
    halves = breadth // LANES
    lines = layers * rows
    opens = (lax.axis_index("gx") == 0).astype(jnp.float32)
    copies = [
        [
            pltpu.make_async_copy(
                far.at[:, h * LANES : (h + 1) * LANES], held_at.at[h * lines : (h + 1) * lines, :], arrived.at[h, k]
            )
            for k, (far, held_at) in enumerate(((warm_far, warm), (energy_far, energy), (speed_far, speed)))
        ]
        for h in range(halves)
    ]
    for some in copies:
        for copy in some:
            copy.start()
    for h in range(halves):
        for copy in copies[h]:
            copy.wait()

        def coefficient_at(i):
            warmth = warm[pl.ds(h * lines + i, layers, stride=rows), :]
            return wide([jnp.exp(slope * warmth) for slope in SLOPES])

        def source_at(i):
            where = pl.ds(h * lines + i, layers, stride=rows)
            warmth = warm[where, :]
            return wide([warmth + energy[where, :], speed[where, :] + lifting_push * warmth])

        def keep(i, ratio, partial, reach):
            where = slice((h * rows + i) * layers, (h * rows + i + 1) * layers)
            ratios[where, :] = ratio
            partials[where, :] = partial
            reaches[where, :] = reach

        values = block_sweep(rows, coefficient_at, source_at, span_strength, opens, keep)[:5]
        sides = [(value[:, :LANES], value[:, LANES:]) for value in values]
        sides.append(tuple(warm[pl.ds(h * lines + i, layers, stride=rows), :] for i in (0, rows - 1)))
        for number, (one, other) in enumerate(sides):
            for part, value in enumerate(cross_halves(one, other)):
                start = (h * PAIRS + part) * layers * SPAN_SENT + number
                send[pl.ds(start, layers, stride=SPAN_SENT), :] = value


def span_reduced(blocks, received, fluxes):
    values = [received[pl.ds(number, blocks, stride=SPAN_SENT), :] for number in range(SPAN_SENT)]
    edges = values.pop()
    left = left_half(edges)
    turned = pltpu.roll(edges, LANES // 2, 1)
    slope = jnp.where(left, SLOPES[0], SLOPES[1])
    values += [jnp.exp(slope * jnp.where(left, one, other)) for one, other in ((edges, turned), (turned, edges))]
    low, high = interface_flux(values, span_strength, blocks)
    fluxes[pl.ds(0, blocks, stride=SIDES), :] = low
    fluxes[pl.ds(1, blocks, stride=SIDES), :] = high


def span_back_cross_forward(
    layers, rows, breadth, warm, flux, ratios, partials, reaches,
    send, chunk_fluxes, cross_ratios, cross_partials, cross_reaches, solved, turned, turned_warm,
):
    halves = breadth // LANES
    lines = layers * rows
    group = min(LANES, lines)
    groups = lines // group
    length = breadth // CHUNKS
    for h in range(halves):
        for g in range(groups):
            start = h * lines + g * group
            turned_warm[g * breadth + h * LANES : g * breadth + (h + 1) * LANES, :] = warm[
                start : start + group, :
            ].T
    for h in range(halves):
        low, high = (
            wide(cross_halves(*(
                flux[pl.ds((h * PAIRS + part) * layers * SIDES + side, layers, stride=SIDES), :]
                for part in range(PAIRS)
            )))
            for side in range(SIDES)
        )

        def kept_at(i):
            where = slice((h * rows + i) * layers, (h * rows + i + 1) * layers)
            return ratios[where, :], partials[where, :], reaches[where, :]

        def give(i, answer):
            for pair in range(PAIRS):
                start = (h * PAIRS + pair) * lines + i
                solved[pl.ds(start, layers, stride=rows), :] = answer[
                    :, pair * LANES : (pair + 1) * LANES
                ]

        block_return(rows, kept_at, low, high, give)
        for pair in range(PAIRS):
            for g in range(groups):
                start = (h * PAIRS + pair) * lines + g * group
                target = (pair * groups + g) * breadth + h * LANES
                turned[target : target + LANES, :] = solved[start : start + group, :].T

    def chunk_row(ref, number, t):
        return ref[pl.ds(number * breadth + t, CHUNKS, stride=length), :]

    def coefficient_at(t):
        warmth = [chunk_row(turned_warm, g, t) for g in range(groups)]
        return wide([jnp.exp(slope * w) for slope in SLOPES for w in warmth])

    def source_at(t):
        return wide([chunk_row(turned, number, t) for number in range(PAIRS * groups)])

    def keep(t, ratio, partial, reach):
        where = slice(t * CHUNKS, (t + 1) * CHUNKS)
        cross_ratios[where, :] = ratio
        cross_partials[where, :] = partial
        cross_reaches[where, :] = reach

    leading = lax.broadcasted_iota(jnp.int32, (CHUNKS, PAIRS * lines), 0) == 0
    opens = jnp.where(leading, (lax.axis_index("gy") == 0).astype(jnp.float32), 0.0)
    values = block_sweep(length, coefficient_at, source_at, cross_strength, opens, keep)
    linear, merged = merge_chunks(values, cross_strength, CHUNKS)
    for number, value in enumerate(linear):
        chunk_fluxes[number * CHUNKS : (number + 1) * CHUNKS, :] = value
    for number, value in enumerate(merged + merged[-1:]):
        send[number : number + 1, :] = value


def cross_pair(mine, partner, merged):
    even = lax.rem(lax.axis_index("gy"), 2) == 0
    lower = jnp.where(even, mine[...], partner[...])
    upper = jnp.where(even, partner[...], mine[...])
    low_first, low_last, low_reach, low_cross, low_end, low_q, low_q_last = (
        lower[number : number + 1, :] for number in range(CROSS_SENT)
    )
    high_first, high_last, high_reach, high_cross, high_end, high_q, high_q_last = (
        upper[number : number + 1, :] for number in range(CROSS_SENT)
    )
    face = 0.5 * cross_strength * (low_q_last + high_q)
    scale = face / (1.0 + face * (low_end + high_reach))
    fixed = scale * (low_last - high_first)
    by_low = scale * low_cross
    by_high = scale * high_cross
    values = (
        low_first - low_cross * fixed,
        high_last + high_cross * fixed,
        low_reach - low_cross * by_low,
        high_cross * by_low,
        high_end - high_cross * by_high,
        low_q,
        high_q_last,
        high_q_last,
    )
    for number, value in enumerate(values):
        merged[number : number + 1, :] = value


def cross_back_depth(
    layers, rows, breadth, warm, *refs
):
    received, refs = refs[:TRADED], refs[TRADED:]
    chunk_fluxes, ratios, partials, reaches, new_warmth, new_speed = refs[:6]
    ordered, turned, solved, depth_ratios, depth_partials, *finished = refs[6:]
    left = finished.pop()
    copies = []
    halves = breadth // LANES
    lines = layers * rows
    group = min(LANES, lines)
    groups = lines // group
    length = breadth // CHUNKS
    own = lax.axis_index("gy")
    in_upper = own // 2
    place = in_upper + lax.rem(own, 2)
    slots = (place, in_upper + 1 - lax.rem(own, 2), 2 - 2 * in_upper)
    for slot, block in zip(slots, received):
        ordered[pl.ds(pl.multiple_of(slot * SENT, SENT), SENT), :] = block[...]
    parts_values = [
        [ordered[d * SENT + number : d * SENT + number + 1, :] for number in range(CROSS_SENT)]
        for d in range(TRADED)
    ]
    end_low, end_high = own_flux(parts_values, cross_strength, place)
    fixed, by_low, by_high = (
        chunk_fluxes[number * CHUNKS : (number + 1) * CHUNKS, :] for number in range(3)
    )
    high = fixed + by_low * end_low + by_high * end_high
    row = lax.broadcasted_iota(jnp.int32, high.shape, 0)
    low = jnp.where(row > 0, pltpu.roll(high, 1, 0), end_low)

    def kept_at(t):
        where = slice(t * CHUNKS, (t + 1) * CHUNKS)
        return ratios[where, :], partials[where, :], reaches[where, :]

    def give(t, answer):
        for number in range(PAIRS * groups):
            turned[pl.ds(number * breadth + t, CHUNKS, stride=length), :] = answer[
                :, number * group : (number + 1) * group
            ]

    block_return(length, kept_at, low, high, give)
    for number in range(PAIRS * groups):
        for h in range(halves):
            start = number * breadth + h * LANES
            solved[number * group : (number + 1) * group, h * LANES : (h + 1) * LANES] = turned[
                start : start + LANES, :
            ].T
    for pair, (far, out) in enumerate(zip((new_warmth, new_speed), finished)):
        half = 0.5 * depth_strength

        def coefficient_at(z):
            starts = [h * lines + z * rows for h in range(halves)]
            return jnp.exp(SLOPES[pair] * wide([warm[start : start + rows, :] for start in starts]))

        def source_at(z):
            return solved[pair * lines + z * rows : pair * lines + (z + 1) * rows, :]

        q_now = coefficient_at(0)
        numerator = source_at(0)
        delta = 1.0 + half * q_now
        for z in range(layers - 1):
            where = slice(z * rows, (z + 1) * rows)
            q_next = coefficient_at(z + 1)
            face = half * (q_now + q_next)
            inverse = 1.0 / (delta + face)
            ratio = face * inverse
            partial = numerator * inverse
            depth_ratios[where, :] = ratio
            depth_partials[where, :] = partial
            delta = 1.0 + delta * ratio
            numerator = source_at(z + 1) + face * partial
            q_now = q_next
        answer = numerator / (delta + half * q_now)
        out[(layers - 1) * rows : layers * rows, :] = answer
        for z in reversed(range(layers - 1)):
            where = slice(z * rows, (z + 1) * rows)
            answer = depth_partials[where, :] + depth_ratios[where, :] * answer
            out[where, :] = answer
            if z % PIECE == 0:
                piece = pl.ds(z * rows, PIECE * rows)
                copies.append(
                    pltpu.make_async_copy(out.at[piece, :], far.at[piece, :], left.at[pair, z // PIECE])
                )
                copies[-1].start()
    for copy in copies:
        copy.wait()


def shaped(*shape):
    return jax.ShapeDtypeStruct(shape, jnp.float32)


def held(*shape):
    return pltpu.VMEM(shape, jnp.float32)


def passed(*shape):
    return pltpu.VMEM(shape, jnp.float32)


def distant(*values):
    return [pltpu.with_memory_space_constraint(value, pltpu.HBM) for value in values]


def near(*values):
    return [pltpu.with_memory_space_constraint(value, pltpu.VMEM) for value in values]


INTERPRET = False


def body(prior_warmth, prior_speed, energy_input):
    layers, rows, breadth = prior_warmth.shape
    lines = layers * rows
    halves = breadth // LANES
    group = min(LANES, lines)
    blocks = lax.axis_size("gx")
    parts = lax.axis_size("gy")
    warm, speed, energy = (v.reshape(lines, breadth) for v in (prior_warmth, prior_speed, energy_input))
    kept = passed(halves * lines, PAIRS * LANES)
    column = (halves * lines, LANES)
    far = pl.BlockSpec(memory_space=pltpu.HBM)
    send, warm, ratios, partials, reaches = pl.pallas_call(
        functools.partial(span_forward, layers, rows, breadth),
        in_specs=[far] * 3,
        out_shape=(passed(blocks * SPAN_SENT, LANES), passed(*column), kept, kept, kept),
        scratch_shapes=[held(*column), held(*column), pltpu.SemaphoreType.DMA((halves, 3))],
        name="span_forward",
        compiler_params=pltpu.CompilerParams(vmem_limit_bytes=ROOM),
        interpret=INTERPRET,
    )(*distant(warm, speed, energy))
    received = lax.all_to_all(
        send.reshape(-1, SIDES, LANES), "gx", split_axis=0, concat_axis=0, tiled=True
    )
    flux = pl.pallas_call(
        functools.partial(span_reduced, blocks),
        out_shape=passed(blocks * SIDES, LANES),
        name="span_reduced",
        compiler_params=pltpu.CompilerParams(vmem_limit_bytes=ROOM),
        interpret=INTERPRET,
    )(*near(received.reshape(blocks * SPAN_SENT, LANES)))
    flux = lax.all_to_all(
        flux.reshape(blocks, SIDES, LANES), "gx", split_axis=0, concat_axis=0, tiled=True
    ).reshape(blocks * SIDES, LANES)
    kept = passed(breadth, PAIRS * lines)
    send, chunk_fluxes, *cross_kept = pl.pallas_call(
        functools.partial(span_back_cross_forward, layers, rows, breadth),
        out_shape=(
            passed(SENT, PAIRS * lines), passed(3 * CHUNKS, PAIRS * lines), kept, kept, kept,
        ),
        scratch_shapes=[
            held(halves * PAIRS * lines, LANES),
            held(PAIRS * lines // group * breadth, group),
            held(lines // group * breadth, group),
        ],
        name="span_back_cross_forward",
        compiler_params=pltpu.CompilerParams(vmem_limit_bytes=ROOM),
        interpret=INTERPRET,
    )(*near(warm, flux, ratios, partials, reaches))
    partner = lax.ppermute(send, "gy", [(i, i ^ 1) for i in range(parts)])
    pair_block = pl.pallas_call(
        cross_pair,
        out_shape=passed(SENT, PAIRS * lines),
        name="cross_pair",
        compiler_params=pltpu.CompilerParams(vmem_limit_bytes=ROOM),
        interpret=INTERPRET,
    )(*near(send, partner))
    other_pair = lax.ppermute(pair_block, "gy", [(i, i ^ 3) for i in range(parts)])
    received = [send, partner, other_pair]
    out = shaped(lines, breadth)
    finished = pl.pallas_call(
        functools.partial(cross_back_depth, layers, rows, breadth),
        out_shape=(out, out),
        out_specs=(far, far),
        scratch_shapes=[
            held(TRADED * SENT, PAIRS * lines),
            held(PAIRS * lines // group * breadth, group),
            held(PAIRS * lines, breadth),
            held(lines, breadth),
            held(lines, breadth),
            held(lines, breadth),
            held(lines, breadth),
            pltpu.SemaphoreType.DMA((PAIRS, layers // PIECE)),
        ],
        name="cross_back_depth",
        compiler_params=pltpu.CompilerParams(vmem_limit_bytes=ROOM),
        interpret=INTERPRET,
    )(*near(warm, *received, chunk_fluxes, *cross_kept))
    return tuple(v.reshape(layers, rows, breadth) for v in finished)


def solution(mesh):
    in_specs = (P(None, "gx", "gy"), P(None, "gx", "gy"), P(None, "gx", "gy"))
    out_specs = (P(None, "gx", "gy"), P(None, "gx", "gy"))
    return jax.shard_map(body, mesh=mesh, in_specs=in_specs, out_specs=out_specs, check_vma=False)
```

```python
import functools

import jax
import jax.numpy as jnp
from jax import lax
from jax.experimental import pallas as pl
from jax.experimental.pallas import tpu as pltpu
from jax.sharding import PartitionSpec as P

diffusivity_slope = 0.3
stickiness_slope = 0.8
lifting_push = 8.0
span_strength = 1500.0
cross_strength = 1500.0
depth_strength = 2.0

SLOPES = (diffusivity_slope, -stickiness_slope)
PAIRS = 2
LANES = 128
CHUNKS = 8
SENT = 8
SIDES = 2
SPAN_SENT = 6
PIECE = 4
ROOM = 24 * 2**20
CROSS_SENT = 7


def block_sweep(steps, coefficient_at, source_at, strength, opens, keep):
    half = 0.5 * strength
    q_first = q_now = coefficient_at(0)
    numerator = source_at(0)
    delta = 1.0 + opens * (half * q_first)
    weight = jnp.ones_like(q_now)
    first_part = jnp.zeros_like(q_now)
    first_reach = jnp.zeros_like(q_now)
    for step in range(steps):
        if step == steps - 1:
            inverse = 1.0 / delta
            partial = numerator * inverse
            reach = weight * inverse
            keep(step, inverse, partial, reach)
            first_part = first_part + weight * partial
            first_reach = first_reach + weight * reach
            return (first_part, partial, first_reach, reach, inverse, q_first, q_now)
        q_next = coefficient_at(step + 1)
        face = half * (q_now + q_next)
        inverse = 1.0 / (delta + face)
        ratio = face * inverse
        partial = numerator * inverse
        reach = weight * inverse
        keep(step, ratio, partial, reach)
        first_part = first_part + weight * partial
        first_reach = first_reach + weight * reach
        delta = 1.0 + delta * ratio
        weight = weight * ratio
        numerator = source_at(step + 1) + face * partial
        q_now = q_next


def block_return(steps, kept_at, flux_low, flux_high, give):
    answer = None
    for step in reversed(range(steps)):
        ratio, partial, reach = kept_at(step)
        fixed = partial + reach * flux_low
        answer = fixed - ratio * flux_high if answer is None else fixed + ratio * answer
        give(step, answer)


def interface_flux(values, strength, rows):
    first_part, last_part, first_reach, cross_reach, last_reach, q_first, q_last = values
    row = lax.broadcasted_iota(jnp.int32, first_part.shape, 0)

    def following(value):
        return jnp.where(row < rows - 1, pltpu.roll(value, rows - 1, 0), 0.0)

    face = 0.5 * strength * (q_last + following(q_first))
    scale = face / (1.0 + face * (last_reach + following(first_reach)))
    below = jnp.where(row > 0, scale * cross_reach, 0.0)
    above = scale * following(cross_reach)
    flux = scale * (last_part - following(first_part))
    step = 1
    while step < rows:
        below_low, above_low, flux_low = (pltpu.roll(v, step, 0) for v in (below, above, flux))
        below_high, above_high, flux_high = (
            pltpu.roll(v, rows - step, 0) for v in (below, above, flux)
        )
        inverse = 1.0 / (1.0 - below * above_low - above * below_high)
        flux = (flux + below * flux_low + above * flux_high) * inverse
        below = below * below_low * inverse
        above = above * above_high * inverse
        step *= 2
    return jnp.where(row > 0, pltpu.roll(flux, 1, 0), 0.0), flux


def merge_chunks(values, strength, rows):
    first_part, last_part, first_reach, cross_reach, last_reach, q_first, q_last = values
    row = lax.broadcasted_iota(jnp.int32, first_part.shape, 0)

    def following(value):
        return pltpu.roll(value, rows - 1, 0)

    def preceding(value):
        return pltpu.roll(value, 1, 0)

    face = 0.5 * strength * (q_last + following(q_first))
    scale = face / (1.0 + face * (last_reach + following(first_reach)))
    scale = jnp.where(row < rows - 1, scale, 0.0)
    below = scale * cross_reach
    above = scale * following(cross_reach)
    fixed = scale * (last_part - following(first_part))
    by_low = jnp.where(row == 0, below, 0.0)
    by_high = jnp.where(row == rows - 2, above, 0.0)
    below = jnp.where(row > 0, below, 0.0)
    above = jnp.where(row < rows - 2, above, 0.0)
    step = 1
    while step < rows:
        lows = [pltpu.roll(v, step, 0) for v in (below, above, fixed, by_low, by_high)]
        highs = [pltpu.roll(v, rows - step, 0) for v in (below, above, fixed, by_low, by_high)]
        inverse = 1.0 / (1.0 - below * lows[1] - above * highs[0])
        fixed, by_low, by_high = (
            (now + below * low + above * high) * inverse
            for now, low, high in zip((fixed, by_low, by_high), lows[2:], highs[2:])
        )
        below = below * lows[0] * inverse
        above = above * highs[1] * inverse
        step *= 2
    by_high = jnp.where(row < rows - 1, by_high, 1.0)
    merged = (
        (first_part - cross_reach * fixed, 0),
        (last_part + cross_reach * preceding(fixed), rows - 1),
        (first_reach - cross_reach * by_low, 0),
        (cross_reach * preceding(by_low), rows - 1),
        (last_reach - cross_reach * preceding(by_high), rows - 1),
        (q_first, 0),
        (q_last, rows - 1),
    )
    return (fixed, by_low, by_high), [value[at : at + 1, :] for value, at in merged]


def own_flux(parts_values, strength, own):
    half = 0.5 * strength
    ratios, fluxes = [], []
    for j, (_, last_part, _, cross_reach, last_reach, _, q_last) in enumerate(parts_values):
        if j + 1 < len(parts_values):
            first_part, _, first_reach, next_cross, _, q_first, _ = parts_values[j + 1]
            face = half * (q_last + q_first)
            centre = 1.0 + face * (last_reach + first_reach)
            right = face * (last_part - first_part)
            above = face * next_cross
        else:
            face = half * q_last
            centre = 1.0 + face * last_reach
            right = face * last_part
            above = None
        if j:
            below = face * cross_reach
            centre = centre - below * ratios[-1]
            right = right + below * fluxes[-1]
        inverse = 1.0 / centre
        fluxes.append(right * inverse)
        ratios.append(None if above is None else above * inverse)
    high = flux = fluxes[-1]
    low = jnp.zeros_like(flux)
    for j in reversed(range(len(fluxes) - 1)):
        flux = fluxes[j] + ratios[j] * flux
        low = jnp.where(own == j + 1, flux, low)
        high = jnp.where(own == j, flux, high)
    return low, high


def left_half(like):
    return lax.broadcasted_iota(jnp.int32, like.shape, 1) < LANES // 2


def cross_halves(one, other):
    left = left_half(one)
    return (
        jnp.where(left, one, pltpu.roll(other, LANES // 2, 1)),
        jnp.where(left, pltpu.roll(one, LANES // 2, 1), other),
    )


def wide(pieces):
    return jnp.concatenate(pieces, axis=1)


def span_forward(
    layers, rows, breadth, warm_far, speed_far, energy_far,
    send, warm, ratios, partials, reaches, speed, energy, arrived,
):
    halves = breadth // LANES
    lines = layers * rows
    opens = (lax.axis_index("gx") == 0).astype(jnp.float32)
    copies = [
        [
            pltpu.make_async_copy(
                far.at[:, h * LANES : (h + 1) * LANES], held_at.at[h * lines : (h + 1) * lines, :], arrived.at[h, k]
            )
            for k, (far, held_at) in enumerate(((warm_far, warm), (energy_far, energy), (speed_far, speed)))
        ]
        for h in range(halves)
    ]
    for some in copies:
        for copy in some:
            copy.start()
    for h in range(halves):
        for copy in copies[h]:
            copy.wait()

        def coefficient_at(i):
            warmth = warm[pl.ds(h * lines + i, layers, stride=rows), :]
            return wide([jnp.exp(slope * warmth) for slope in SLOPES])

        def source_at(i):
            where = pl.ds(h * lines + i, layers, stride=rows)
            warmth = warm[where, :]
            return wide([warmth + energy[where, :], speed[where, :] + lifting_push * warmth])

        def keep(i, ratio, partial, reach):
            where = slice((h * rows + i) * layers, (h * rows + i + 1) * layers)
            ratios[where, :] = ratio
            partials[where, :] = partial
            reaches[where, :] = reach

        values = block_sweep(rows, coefficient_at, source_at, span_strength, opens, keep)[:5]
        sides = [(value[:, :LANES], value[:, LANES:]) for value in values]
        sides.append(tuple(warm[pl.ds(h * lines + i, layers, stride=rows), :] for i in (0, rows - 1)))
        for number, (one, other) in enumerate(sides):
            for part, value in enumerate(cross_halves(one, other)):
                start = (h * PAIRS + part) * layers * SPAN_SENT + number
                send[pl.ds(start, layers, stride=SPAN_SENT), :] = value


def span_reduced(blocks, received, fluxes):
    values = [received[pl.ds(number, blocks, stride=SPAN_SENT), :] for number in range(SPAN_SENT)]
    edges = values.pop()
    left = left_half(edges)
    turned = pltpu.roll(edges, LANES // 2, 1)
    slope = jnp.where(left, SLOPES[0], SLOPES[1])
    values += [jnp.exp(slope * jnp.where(left, one, other)) for one, other in ((edges, turned), (turned, edges))]
    low, high = interface_flux(values, span_strength, blocks)
    fluxes[pl.ds(0, blocks, stride=SIDES), :] = low
    fluxes[pl.ds(1, blocks, stride=SIDES), :] = high


def span_back_cross_forward(
    layers, rows, breadth, warm, flux, ratios, partials, reaches,
    send, chunk_fluxes, cross_ratios, cross_partials, cross_reaches, solved, turned, turned_warm,
):
    halves = breadth // LANES
    lines = layers * rows
    group = min(LANES, lines)
    groups = lines // group
    length = breadth // CHUNKS
    for h in range(halves):
        for g in range(groups):
            start = h * lines + g * group
            turned_warm[g * breadth + h * LANES : g * breadth + (h + 1) * LANES, :] = warm[
                start : start + group, :
            ].T
    for h in range(halves):
        low, high = (
            wide(cross_halves(*(
                flux[pl.ds((h * PAIRS + part) * layers * SIDES + side, layers, stride=SIDES), :]
                for part in range(PAIRS)
            )))
            for side in range(SIDES)
        )

        def kept_at(i):
            where = slice((h * rows + i) * layers, (h * rows + i + 1) * layers)
            return ratios[where, :], partials[where, :], reaches[where, :]

        def give(i, answer):
            for pair in range(PAIRS):
                start = (h * PAIRS + pair) * lines + i
                solved[pl.ds(start, layers, stride=rows), :] = answer[
                    :, pair * LANES : (pair + 1) * LANES
                ]

        block_return(rows, kept_at, low, high, give)
        for pair in range(PAIRS):
            for g in range(groups):
                start = (h * PAIRS + pair) * lines + g * group
                target = (pair * groups + g) * breadth + h * LANES
                turned[target : target + LANES, :] = solved[start : start + group, :].T

    def chunk_row(ref, number, t):
        return ref[pl.ds(number * breadth + t, CHUNKS, stride=length), :]

    def coefficient_at(t):
        warmth = [chunk_row(turned_warm, g, t) for g in range(groups)]
        return wide([jnp.exp(slope * w) for slope in SLOPES for w in warmth])

    def source_at(t):
        return wide([chunk_row(turned, number, t) for number in range(PAIRS * groups)])

    def keep(t, ratio, partial, reach):
        where = slice(t * CHUNKS, (t + 1) * CHUNKS)
        cross_ratios[where, :] = ratio
        cross_partials[where, :] = partial
        cross_reaches[where, :] = reach

    leading = lax.broadcasted_iota(jnp.int32, (CHUNKS, PAIRS * lines), 0) == 0
    opens = jnp.where(leading, (lax.axis_index("gy") == 0).astype(jnp.float32), 0.0)
    values = block_sweep(length, coefficient_at, source_at, cross_strength, opens, keep)
    linear, merged = merge_chunks(values, cross_strength, CHUNKS)
    for number, value in enumerate(linear):
        chunk_fluxes[number * CHUNKS : (number + 1) * CHUNKS, :] = value
    for number, value in enumerate(merged + merged[-1:]):
        send[number : number + 1, :] = value


def depth_factors(layers, rows, breadth, warm, chunk_fluxes, inverses, ratios, carries):
    halves = breadth // LANES
    lines = layers * rows
    half = 0.5 * depth_strength
    for pair in range(PAIRS):

        def coefficient_at(z):
            starts = [h * lines + z * rows for h in range(halves)]
            return jnp.exp(SLOPES[pair] * wide([warm[start : start + rows, :] for start in starts]))

        q_now = coefficient_at(0)
        delta = 1.0 + half * q_now
        face_before = None
        for z in range(layers):
            where = slice(pair * lines + z * rows, pair * lines + (z + 1) * rows)
            if z < layers - 1:
                q_next = coefficient_at(z + 1)
                face = half * (q_now + q_next)
            else:
                q_next, face = q_now, half * q_now
            inverse = 1.0 / (delta + face)
            inverses[where, :] = inverse
            if face_before is not None:
                carries[where, :] = face_before * inverse
            ratio = face * inverse
            if z < layers - 1:
                ratios[where, :] = ratio
                delta = 1.0 + delta * ratio
            q_now, face_before = q_next, face


def cross_back_depth(
    layers, rows, breadth, parts, *refs
):
    received, refs = refs[:parts], refs[parts:]
    chunk_fluxes, ratios, partials, reaches = refs[:4]
    depth_inverses, depth_ratios, depth_carries, new_warmth, new_speed = refs[4:9]
    ordered, turned, solved, depth_partials, *finished = refs[9:]
    left = finished.pop()
    copies = []
    halves = breadth // LANES
    lines = layers * rows
    group = min(LANES, lines)
    groups = lines // group
    length = breadth // CHUNKS
    own = lax.axis_index("gy")
    for number, steps in enumerate(range(parts)):
        slot = lax.rem(own + parts - steps, parts)
        ordered[pl.ds(pl.multiple_of(slot * SENT, SENT), SENT), :] = received[number][...]
    parts_values = [
        [ordered[d * SENT + number : d * SENT + number + 1, :] for number in range(CROSS_SENT)]
        for d in range(parts)
    ]
    end_low, end_high = own_flux(parts_values, cross_strength, own)
    fixed, by_low, by_high = (
        chunk_fluxes[number * CHUNKS : (number + 1) * CHUNKS, :] for number in range(3)
    )
    high = fixed + by_low * end_low + by_high * end_high
    row = lax.broadcasted_iota(jnp.int32, high.shape, 0)
    low = jnp.where(row > 0, pltpu.roll(high, 1, 0), end_low)

    def kept_at(t):
        where = slice(t * CHUNKS, (t + 1) * CHUNKS)
        return ratios[where, :], partials[where, :], reaches[where, :]

    def give(t, answer):
        for number in range(PAIRS * groups):
            turned[pl.ds(number * breadth + t, CHUNKS, stride=length), :] = answer[
                :, number * group : (number + 1) * group
            ]

    block_return(length, kept_at, low, high, give)
    for number in range(PAIRS * groups):
        for h in range(halves):
            start = number * breadth + h * LANES
            solved[number * group : (number + 1) * group, h * LANES : (h + 1) * LANES] = turned[
                start : start + LANES, :
            ].T
    for pair, (far, out) in enumerate(zip((new_warmth, new_speed), finished)):
        base = pair * lines
        partial = None
        for z in range(layers):
            where = slice(base + z * rows, base + (z + 1) * rows)
            fixed = solved[where, :] * depth_inverses[where, :]
            partial = fixed if partial is None else fixed + depth_carries[where, :] * partial
            if z < layers - 1:
                depth_partials[z * rows : (z + 1) * rows, :] = partial
        answer = partial
        out[(layers - 1) * rows : layers * rows, :] = answer
        for z in reversed(range(layers - 1)):
            where = slice(z * rows, (z + 1) * rows)
            ratio = depth_ratios[base + z * rows : base + (z + 1) * rows, :]
            answer = depth_partials[where, :] + ratio * answer
            out[where, :] = answer
            if z % PIECE == 0:
                piece = pl.ds(z * rows, PIECE * rows)
                copies.append(
                    pltpu.make_async_copy(out.at[piece, :], far.at[piece, :], left.at[pair, z // PIECE])
                )
                copies[-1].start()
    for copy in copies:
        copy.wait()


def shaped(*shape):
    return jax.ShapeDtypeStruct(shape, jnp.float32)


def held(*shape):
    return pltpu.VMEM(shape, jnp.float32)


def passed(*shape):
    return pltpu.VMEM(shape, jnp.float32)


def distant(*values):
    return [pltpu.with_memory_space_constraint(value, pltpu.HBM) for value in values]


def near(*values):
    return [pltpu.with_memory_space_constraint(value, pltpu.VMEM) for value in values]


INTERPRET = False


def body(prior_warmth, prior_speed, energy_input):
    layers, rows, breadth = prior_warmth.shape
    lines = layers * rows
    halves = breadth // LANES
    group = min(LANES, lines)
    blocks = lax.axis_size("gx")
    parts = lax.axis_size("gy")
    warm, speed, energy = (v.reshape(lines, breadth) for v in (prior_warmth, prior_speed, energy_input))
    kept = passed(halves * lines, PAIRS * LANES)
    column = (halves * lines, LANES)
    far = pl.BlockSpec(memory_space=pltpu.HBM)
    send, warm, ratios, partials, reaches = pl.pallas_call(
        functools.partial(span_forward, layers, rows, breadth),
        in_specs=[far] * 3,
        out_shape=(passed(blocks * SPAN_SENT, LANES), passed(*column), kept, kept, kept),
        scratch_shapes=[held(*column), held(*column), pltpu.SemaphoreType.DMA((halves, 3))],
        name="span_forward",
        compiler_params=pltpu.CompilerParams(vmem_limit_bytes=ROOM),
        interpret=INTERPRET,
    )(*distant(warm, speed, energy))
    received = lax.all_to_all(
        send.reshape(-1, SIDES, LANES), "gx", split_axis=0, concat_axis=0, tiled=True
    )
    flux = pl.pallas_call(
        functools.partial(span_reduced, blocks),
        out_shape=passed(blocks * SIDES, LANES),
        name="span_reduced",
        compiler_params=pltpu.CompilerParams(vmem_limit_bytes=ROOM),
        interpret=INTERPRET,
    )(*near(received.reshape(blocks * SPAN_SENT, LANES)))
    flux = lax.all_to_all(
        flux.reshape(blocks, SIDES, LANES), "gx", split_axis=0, concat_axis=0, tiled=True
    ).reshape(blocks * SIDES, LANES)
    kept = passed(breadth, PAIRS * lines)
    send, chunk_fluxes, *cross_kept = pl.pallas_call(
        functools.partial(span_back_cross_forward, layers, rows, breadth),
        out_shape=(
            passed(SENT, PAIRS * lines), passed(3 * CHUNKS, PAIRS * lines), kept, kept, kept,
        ),
        scratch_shapes=[
            held(halves * PAIRS * lines, LANES),
            held(PAIRS * lines // group * breadth, group),
            held(lines // group * breadth, group),
        ],
        name="span_back_cross_forward",
        compiler_params=pltpu.CompilerParams(vmem_limit_bytes=ROOM),
        interpret=INTERPRET,
    )(*near(warm, flux, ratios, partials, reaches))
    received = [
        lax.ppermute(send, "gy", [(i, (i + steps) % parts) for i in range(parts)]) if steps else send
        for steps in range(parts)
    ]
    factors = pl.pallas_call(
        functools.partial(depth_factors, layers, rows, breadth),
        out_shape=(passed(PAIRS * lines, breadth),) * 3,
        name="depth_factors",
        compiler_params=pltpu.CompilerParams(vmem_limit_bytes=ROOM),
        interpret=INTERPRET,
    )(*near(warm, chunk_fluxes))
    out = shaped(lines, breadth)
    finished = pl.pallas_call(
        functools.partial(cross_back_depth, layers, rows, breadth, parts),
        out_shape=(out, out),
        out_specs=(far, far),
        scratch_shapes=[
            held(parts * SENT, PAIRS * lines),
            held(PAIRS * lines // group * breadth, group),
            held(PAIRS * lines, breadth),
            held(lines, breadth),
            held(lines, breadth),
            held(lines, breadth),
            pltpu.SemaphoreType.DMA((PAIRS, layers // PIECE)),
        ],
        name="cross_back_depth",
        compiler_params=pltpu.CompilerParams(vmem_limit_bytes=ROOM),
        interpret=INTERPRET,
    )(*near(*received, chunk_fluxes, *cross_kept, *factors))
    return tuple(v.reshape(layers, rows, breadth) for v in finished)


def solution(mesh):
    in_specs = (P(None, "gx", "gy"), P(None, "gx", "gy"), P(None, "gx", "gy"))
    out_specs = (P(None, "gx", "gy"), P(None, "gx", "gy"))
    return jax.shard_map(body, mesh=mesh, in_specs=in_specs, out_specs=out_specs, check_vma=False)
```
